32 devices in a mesh: seq: 8 (over y, x, core), head: 4 (over z).
Axes of the slice: x: 2, y: 2, z: 4, core: 2. Of those that a mesh axis runs over, the one named last changes fastest.
Arguments:
- projected: bfloat16 [4096, 3, 3072], P(('seq', 'head')), may hold values from -70 to 70
- key_lists: int32 [48, 32, 8], P('head', 'seq'), may hold values from 0 to 31, as said below
- list_counts: int32 [48, 32], P('head', 'seq'), may hold values from 1 to 8
Outputs:
- attended: bfloat16 [4096, 3072], P(('seq', 'head'))
The draws below stay inside these ranges and needn't reach their ends.
Inputs may be any that keep to these rules, and one draw needn't show every extreme that they name: `key_lists`: entries are key block numbers; no list names its own query block, and the entries of one list are distinct. Entry j of the list of query block b in head h lies on seq shard (b // 4 + o + j) mod 8, o depending on h and b. Over the 12 heads of one head group and the query blocks of one seq shard, exactly 48 entries lie on each seq shard, entries past a list's count included, and the entries that lie on one seq shard name at most two distinct key blocks: at most one whose number within its shard is below 2 and at most one whose number is at least that. In every draw some head group, seq shard and owning seq shard have two.
All inputs are finite; a program needn't handle non-finite values.
Results may differ from the reference program's by a relative error of at most 0.005.
Values may be sent and summed in bfloat16 or wider, within the bound.
No kernel may reach another device: no remote copies, remote signals or barrier semaphores. Data moves between devices by JAX's collectives and lax.ppermute only.
A program may use at most 128 MiB of HBM per device.

```python
import math
import jax
import jax.numpy as jnp
from jax import lax

HEADS = 48
HD = 64
BLK = 128
KMAX = 8
HPD = 12
QB_DEV = 4
NB = 32
TOKENS = 4096
N_SEQ = 8
N_HEAD = 4


def draw_key_lists(key, part):
    row_count = HPD * QB_DEV
    half_count = QB_DEV // 2

    def one_device(device_key, seq_index):
        order = jax.random.permutation(jax.random.fold_in(device_key, 1), row_count).astype(jnp.int32)
        first_value = order[0]
        partner = jnp.bitwise_xor(first_value, 1).astype(jnp.int32)
        where_partner = jnp.argmax(order == partner).astype(jnp.int32)
        moved_value = order[half_count]
        order = order.at[where_partner].set(moved_value)
        order = order.at[half_count].set(partner)
        offsets = order * N_SEQ // row_count
        column = jnp.arange(KMAX, dtype=jnp.int32)
        owners = (seq_index + offsets[:, None] + column[None, :]) % N_SEQ
        query_local = (jnp.arange(row_count, dtype=jnp.int32) % QB_DEV)[:, None]
        lower_half = query_local // half_count
        picks = jax.random.randint(jax.random.fold_in(device_key, 3), (N_SEQ,), 0, half_count).astype(jnp.int32)
        owner_pick = jnp.take(picks, owners, axis=0)
        half_bit = jnp.where(owners == seq_index, 1 - lower_half, lower_half)
        local_block = half_bit * half_count + owner_pick
        return (owners * QB_DEV + local_block).astype(jnp.int32).reshape(HPD, QB_DEV, KMAX)
    device_ids = jnp.arange(N_SEQ * N_HEAD, dtype=jnp.int32)
    device_keys = jax.vmap(lambda number: jax.random.fold_in(key, number))(device_ids)
    drawn = jax.vmap(one_device)(device_keys, device_ids // N_HEAD)
    drawn = drawn.reshape(N_SEQ, N_HEAD, HPD, QB_DEV, KMAX).transpose(1, 2, 0, 3, 4)
    return drawn.reshape(HEADS, NB, KMAX)


def draw_list_counts(key, part):
    spans = jax.random.randint(jax.random.fold_in(key, 11), (HEADS, 1), 0, KMAX)
    raw_counts = 1 + jax.random.randint(jax.random.fold_in(key, 12), (HEADS, NB), 0, KMAX) % (spans + 1)
    block_ids = jnp.arange(NB, dtype=jnp.int32)[None, :]
    low_block = jax.random.randint(jax.random.fold_in(key, 13), (HEADS, 1), 0, NB)
    high_block = jax.random.randint(jax.random.fold_in(key, 14), (HEADS, 1), 0, NB)
    raw_counts = jnp.where(block_ids == low_block, 1, raw_counts)
    raw_counts = jnp.where(block_ids == high_block, KMAX, raw_counts)
    return raw_counts.astype(jnp.int32)


def draw_projected(key, part):
    shape = (TOKENS, 3, HEADS * HD)
    return jnp.clip(jax.random.normal(jax.random.fold_in(key, 21), shape, jnp.float32), -6.0, 6.0).astype(jnp.bfloat16)


def setup_inputs(seed: int = 0) -> dict:
    keys = jax.random.split(jax.random.key(seed), 4)
    projected = draw_projected(jax.random.fold_in(keys[3], 71), 0)
    key_lists = draw_key_lists(jax.random.fold_in(keys[3], 71), 0)
    list_counts = draw_list_counts(jax.random.fold_in(keys[3], 71), 0)
    return {"projected": projected, "key_lists": key_lists, "list_counts": list_counts}


NEG_FILL = -1e+30

def reference(projected, key_lists, list_counts):
    token_count = projected.shape[0]
    block_total = token_count // BLK
    splitted = projected.reshape(block_total, BLK, 3, HEADS, HD)
    logit_scale = 1.0 / math.sqrt(HD)
    queries = splitted[:, :, 0].transpose(2, 0, 1, 3)
    key_rows = splitted[:, :, 1].transpose(2, 0, 1, 3)
    value_rows = splitted[:, :, 2].transpose(2, 0, 1, 3)
    block_ids = jnp.arange(block_total, dtype=jnp.int32)[:, None]

    def one_head(inputs):
        query_for_head, head_key, head_value, head_lists, head_counts = inputs
        seen_blocks = jnp.concatenate([block_ids, head_lists.astype(jnp.int32)], axis=1)
        live_cols = jnp.concatenate([jnp.ones((block_total, 1), bool), jnp.arange(KMAX, dtype=jnp.int32)[None, :] < head_counts[:, None]], axis=1)
        nearby_keys = head_key[seen_blocks].reshape(block_total, (KMAX + 1) * BLK, HD)
        nearby_values = head_value[seen_blocks].reshape(block_total, (KMAX + 1) * BLK, HD)
        attention_scores = jnp.einsum('opn,oen->ope', query_for_head.astype(jnp.float32), nearby_keys.astype(jnp.float32)) * logit_scale
        attention_scores = attention_scores.reshape(block_total, BLK, KMAX + 1, BLK)
        attention_scores = jnp.where(live_cols[:, None, :, None], attention_scores, NEG_FILL)
        row_top = lax.optimization_barrier(jnp.max(attention_scores, axis=(2, 3), keepdims=True))
        exp_scores = jnp.exp(attention_scores - row_top)
        attention_weights = (exp_scores / lax.optimization_barrier(jnp.sum(exp_scores, axis=(2, 3), keepdims=True))).astype(jnp.bfloat16)
        attention_weights = lax.optimization_barrier(attention_weights).astype(jnp.float32).reshape(block_total, BLK, (KMAX + 1) * BLK)
        weighted_sum = jnp.einsum('hep,hps->hes', attention_weights, nearby_values.astype(jnp.float32))
        return weighted_sum.astype(jnp.bfloat16)
    attended = lax.map(one_head, (queries, key_rows, value_rows, key_lists, list_counts))
    return attended.transpose(1, 2, 0, 3).reshape(token_count, HEADS * HD)
```

```python
import functools
import math

import jax
import jax.numpy as jnp
from jax import lax
from jax.experimental import pallas as pl
from jax.experimental.pallas import tpu as pltpu
from jax.sharding import Mesh
from jax.sharding import PartitionSpec as P

NEG_FILL = -1e30
LOG2E = 1.4426950408889634
PAIR = 2
ROWS = 4
STEP = 3
SUM_ROWS = 16


def pack_kernel(q_ref, k_ref, v_ref, out_ref, *, per_chip, head_size):
    tokens = q_ref.shape[0]
    half = tokens // 2
    lanes = 2 * head_size
    for pair in range(q_ref.shape[1] // lanes):
        cols = slice(pair * lanes, (pair + 1) * lanes)
        q_t = q_ref[:, cols].T
        v_t = v_ref[:, cols].T
        k_tile = k_ref[:, cols]
        for odd in range(2):
            chip, j = divmod(2 * pair + odd, per_chip)
            part = slice(odd * head_size, (odd + 1) * head_size)
            out_ref[chip, j, 0] = q_t[part]
            out_ref[chip, j, 1] = jnp.concatenate([k_tile[:half, part], k_tile[half:, part]], axis=1)
            out_ref[chip, j, 2] = v_t[part]


def pack(queries, keys, values, *, chips, per_chip, head_size):
    tokens, width = queries.shape
    steps = 8
    spec = pl.BlockSpec((tokens, width // steps), lambda i: (0, i))
    return pl.pallas_call(
        functools.partial(pack_kernel, per_chip=per_chip, head_size=head_size),
        grid=(steps,),
        in_specs=[spec] * 3,
        out_specs=pl.BlockSpec(
            (chips // steps, per_chip, 3, head_size, tokens), lambda i: (i, 0, 0, 0, 0)
        ),
        out_shape=jax.ShapeDtypeStruct((chips, per_chip, 3, head_size, tokens), queries.dtype),
        name="pack",
    )(queries, keys, values)


def attend_kernel(slots_ref, counts_ref, mine_ref, other_ref, out_ref, kv, total, *, scale, list_most):
    blocks, _, _, head_size, tokens = mine_ref.shape
    head = pl.program_id(0)
    for b in range(blocks):
        kv[b] = mine_ref[b, 0, 1:3]
        kv[blocks + b] = other_ref[b, 0]
    entries = 1 + list_most
    ones = jnp.ones((SUM_ROWS, tokens), jnp.bfloat16)
    zeros = jnp.zeros((head_size, tokens), jnp.bfloat16)

    def group(g, carry):
        base = g * ROWS
        counts = [counts_ref[head * blocks + base + r] for r in range(ROWS)]
        most = functools.reduce(jnp.maximum, counts)
        weights = []
        for r in range(ROWS):
            q_t = mine_ref[base + r, 0, 0]
            weights.append(
                jnp.concatenate(
                    [jnp.concatenate([q_t, zeros], axis=1), jnp.concatenate([zeros, q_t], axis=1)],
                    axis=0,
                )
            )

        def chunk(first, width, old):
            tops, result = [], []
            for r in range(ROWS):
                row = (head * blocks + base + r) * entries
                own = slots_ref[row]
                keys, vals = [], []
                for e in range(first, first + width):
                    if e == 0:
                        slot = own
                        keys.append(kv[slot, 0])
                        vals.append(jnp.concatenate([kv[slot, 1], ones], axis=0))
                    else:
                        live = e <= counts[r]
                        slot = jnp.where(live, slots_ref[row + e], own)
                        factor = jnp.where(live, 1.0, 0.0).astype(jnp.bfloat16)
                        keys.append(kv[slot, 0])
                        vals.append(jnp.concatenate([kv[slot, 1], ones], axis=0) * factor)
                scores = jnp.dot(
                    jnp.concatenate(keys, axis=0), weights[r], preferred_element_type=jnp.float32
                )
                top = jnp.max(scores, axis=0, keepdims=True)
                top = jnp.maximum(top[:, :tokens], top[:, tokens:])
                if old is not None:
                    top = jnp.maximum(top, old[r])
                both = jnp.concatenate([top, top], axis=1)
                probs = jnp.exp2((scores - both) * scale).astype(jnp.bfloat16)
                probs = jnp.concatenate(
                    [
                        probs[w * head_size : (w + 1) * head_size, c * tokens : (c + 1) * tokens]
                        for w in range(width)
                        for c in range(2)
                    ],
                    axis=0,
                )
                part = jnp.dot(
                    jnp.concatenate(vals, axis=1), probs, preferred_element_type=jnp.float32
                )
                if old is not None:
                    part = part + total[r] * jnp.exp2((old[r] - top) * scale)
                total[r] = part
                tops.append(top)
            return tuple(tops)

        tops = chunk(0, STEP, None)
        for first in range(STEP, entries, STEP):
            tops = lax.cond(
                most >= first,
                functools.partial(chunk, first, min(STEP, entries - first)),
                lambda old: old,
                tops,
            )
        for r in range(ROWS):
            whole = total[r]
            out_ref[base + r, 0] = (whole[:head_size] / whole[head_size : head_size + 1]).astype(
                out_ref.dtype
            )
        return carry

    lax.fori_loop(0, blocks // ROWS, group, 0)


def attend(slots, counts, mine, other, *, list_most):
    blocks, per_chip, _, head_size, tokens = mine.shape
    return pl.pallas_call(
        functools.partial(
            attend_kernel, scale=LOG2E / math.sqrt(head_size), list_most=list_most
        ),
        grid_spec=pltpu.PrefetchScalarGridSpec(
            num_scalar_prefetch=2,
            grid=(per_chip,),
            in_specs=[
                pl.BlockSpec((blocks, 1, 3, head_size, tokens), lambda j, s, c: (0, j, 0, 0, 0)),
                pl.BlockSpec((blocks, 1, 2, head_size, tokens), lambda j, s, c: (0, j, 0, 0, 0)),
            ],
            out_specs=pl.BlockSpec((blocks, 1, head_size, tokens), lambda j, s, c: (0, j, 0, 0)),
            scratch_shapes=[
                pltpu.VMEM((2 * blocks, 2, head_size, tokens), jnp.bfloat16),
                pltpu.VMEM((ROWS, head_size + SUM_ROWS, tokens), jnp.float32),
            ],
        ),
        out_shape=jax.ShapeDtypeStruct((blocks, per_chip, head_size, tokens), mine.dtype),
        compiler_params=pltpu.CompilerParams(vmem_limit_bytes=48 << 20),
        name="attend",
    )(slots, counts, mine, other)


def on_pair(projected, key_lists, list_counts, *, chips_seq, head_count):
    tokens, _, width = projected.shape
    heads_dev, blocks_dev, list_most = key_lists.shape
    chips = chips_seq * head_count
    head_size = width // (heads_dev * head_count)
    per_chip = heads_dev // chips_seq
    core = lax.axis_index("core")

    table = jnp.concatenate([key_lists, list_counts[:, :, None]], axis=2)
    table = lax.all_to_all(
        table.reshape(chips_seq, per_chip, blocks_dev, list_most + 1),
        "chip", split_axis=0, concat_axis=0, tiled=True,
    )
    table = table.transpose(1, 2, 0, 3).reshape(per_chip * chips, list_most + 1)
    listed, counts = table[:, :list_most], table[:, list_most]
    shard = listed // blocks_dev
    slots = (
        ((shard % PAIR) != core).astype(jnp.int32) * chips
        + (listed % blocks_dev) * chips_seq
        + shard // PAIR
    )
    own = jnp.arange(per_chip * chips, dtype=jnp.int32)[:, None] % chips
    slots = jnp.concatenate([own, slots], axis=1).reshape(-1)

    packed = pack(
        projected[:, 0], projected[:, 1], projected[:, 2],
        chips=chips, per_chip=per_chip, head_size=head_size,
    )
    mine = lax.all_to_all(packed, ("head", "chip"), split_axis=0, concat_axis=0, tiled=True)
    other = lax.ppermute(mine[:, :, 1:], "core", [(0, 1), (1, 0)])
    attended = attend(slots, counts, mine, other, list_most=list_most)
    back = lax.all_to_all(attended, ("head", "chip"), split_axis=0, concat_axis=0, tiled=True)
    return back.reshape(width, tokens).T


def attend_rows(query_part, gathered, live_cols, head_size):
    row_count, seen_blocks, block_len, doubled = gathered.shape
    key_rows = gathered[..., :head_size].reshape(row_count, seen_blocks * block_len, head_size)
    value_rows = gathered[..., head_size:].reshape(row_count, seen_blocks * block_len, head_size)
    attention_scores = jnp.einsum(
        "rqd,rkd->rqk", query_part, key_rows, preferred_element_type=jnp.float32
    ) * (1.0 / math.sqrt(head_size))
    attention_scores = attention_scores.reshape(row_count, block_len, seen_blocks, block_len)
    attention_scores = jnp.where(live_cols[:, None, :, None], attention_scores, NEG_FILL)
    row_top = jnp.max(attention_scores, axis=(2, 3), keepdims=True)
    exp_scores = jnp.exp(attention_scores - row_top)
    attention_weights = (exp_scores / jnp.sum(exp_scores, axis=(2, 3), keepdims=True)).astype(
        jnp.bfloat16
    )
    attention_weights = attention_weights.reshape(row_count, block_len, seen_blocks * block_len)
    return jnp.einsum(
        "rqk,rkd->rqd", attention_weights, value_rows, preferred_element_type=jnp.float32
    )


def on_device(projected, key_lists, list_counts):
    seq_count = lax.axis_size("seq")
    heads_dev, blocks_dev, list_most = key_lists.shape
    regrouped = lax.all_to_all(projected, "head", split_axis=2, concat_axis=0, tiled=True)
    block_len = regrouped.shape[0] // blocks_dev
    group_width = regrouped.shape[2]
    head_size = group_width // heads_dev
    row_count = heads_dev * blocks_dev
    splitted = regrouped.reshape(blocks_dev, block_len, 3, heads_dev, head_size)
    queries = splitted[:, :, 0].transpose(2, 0, 1, 3).reshape(row_count, block_len, head_size)
    kv_pairs = jnp.concatenate([splitted[:, :, 1], splitted[:, :, 2]], axis=-1)
    kv_pairs = kv_pairs.transpose(2, 0, 1, 3).reshape(row_count, block_len, 2 * head_size)
    entries = key_lists.reshape(row_count * list_most)
    owners = entries // blocks_dev
    row_head = jnp.arange(row_count * list_most, dtype=jnp.int32) // (blocks_dev * list_most)
    capacity = row_count * list_most // seq_count
    wanted = row_head * blocks_dev + entries % blocks_dev
    onehot = (owners[:, None] == jnp.arange(seq_count, dtype=jnp.int32)[None, :]).astype(jnp.int32)
    within = jnp.sum(onehot * (jnp.cumsum(onehot, axis=0) - 1), axis=1)
    slot_ids = owners * capacity + within
    request = (
        jnp.zeros((seq_count * capacity,), jnp.int32)
        .at[slot_ids]
        .set(wanted)
        .reshape(seq_count, capacity)
    )
    asked_for = lax.all_to_all(request, "seq", split_axis=0, concat_axis=0, tiled=True)
    served = jnp.take(kv_pairs, asked_for.reshape(-1), axis=0).reshape(
        seq_count, capacity, block_len, 2 * head_size
    )
    fetched = lax.all_to_all(served, "seq", split_axis=0, concat_axis=0, tiled=True)
    fetched = fetched.reshape(seq_count * capacity, block_len, 2 * head_size)
    entry_slots = slot_ids.reshape(row_count, list_most)
    row_counts = list_counts.reshape(row_count)
    group_rows = 4

    def one_group(group_index):
        start = group_index * group_rows
        query_part = lax.dynamic_slice_in_dim(queries, start, group_rows, 0)
        own_pairs = lax.dynamic_slice_in_dim(kv_pairs, start, group_rows, 0)
        slot_part = lax.dynamic_slice_in_dim(entry_slots, start, group_rows, 0)
        count_part = lax.dynamic_slice_in_dim(row_counts, start, group_rows, 0)
        listed = jnp.take(fetched, slot_part.reshape(-1), axis=0).reshape(
            group_rows, list_most, block_len, 2 * head_size
        )
        gathered = jnp.concatenate([own_pairs[:, None], listed], axis=1)
        live_cols = jnp.concatenate(
            [
                jnp.ones((group_rows, 1), bool),
                jnp.arange(list_most, dtype=jnp.int32)[None, :] < count_part[:, None],
            ],
            axis=1,
        )
        return attend_rows(query_part, gathered, live_cols, head_size).astype(jnp.bfloat16)

    attended = lax.map(one_group, jnp.arange(row_count // group_rows, dtype=jnp.int32))
    attended = attended.reshape(row_count, block_len, head_size)
    laid_out = attended.reshape(heads_dev, blocks_dev * block_len, head_size).transpose(1, 0, 2)
    laid_out = laid_out.reshape(blocks_dev * block_len, group_width)
    return lax.all_to_all(laid_out, "head", split_axis=0, concat_axis=1, tiled=True)


def whole_heads_fit(mesh, projected, key_lists):
    seq_count, head_count = mesh.shape["seq"], mesh.shape["head"]
    if seq_count % PAIR:
        return False
    chips_seq = seq_count // PAIR
    chips = chips_seq * head_count
    group_heads = key_lists.shape[0] // head_count
    one_block = key_lists.shape[1] == seq_count * head_count
    return one_block and group_heads % chips_seq == 0 and chips % 8 == 0 and chips % ROWS == 0


def solution(mesh):
    seq_count, head_count = mesh.shape["seq"], mesh.shape["head"]

    def run(projected, key_lists, list_counts):
        if not whole_heads_fit(mesh, projected, key_lists):
            return jax.shard_map(
                on_device,
                mesh=mesh,
                in_specs=(P(("seq", "head"), None, None), P("head", "seq", None), P("head", "seq")),
                out_specs=P(("seq", "head"), None),
                check_vma=False,
            )(projected, key_lists, list_counts)
        chips_seq = seq_count // PAIR
        split = Mesh(mesh.devices.reshape(chips_seq, PAIR, head_count), ("chip", "core", "head"))
        seq = ("chip", "core")
        return jax.shard_map(
            functools.partial(on_pair, chips_seq=chips_seq, head_count=head_count),
            mesh=split,
            in_specs=(P(seq + ("head",), None, None), P("head", seq, None), P("head", seq)),
            out_specs=P(seq + ("head",), None),
            check_vma=False,
        )(projected, key_lists, list_counts)

    return run
```

```python
import functools
import math

import jax
import jax.numpy as jnp
from jax import lax
from jax.experimental import pallas as pl
from jax.experimental.pallas import tpu as pltpu
from jax.sharding import Mesh
from jax.sharding import PartitionSpec as P

NEG_FILL = -1e30
LOG2E = 1.4426950408889634
PAIR = 2
ROWS = 8
SUM_ROWS = 16


def pack_kernel(q_ref, k_ref, v_ref, out_ref, *, per_chip, head_size):
    tokens = q_ref.shape[0]
    half = tokens // 2
    lanes = 2 * head_size
    for pair in range(q_ref.shape[1] // lanes):
        cols = slice(pair * lanes, (pair + 1) * lanes)
        q_t = q_ref[:, cols].T
        v_t = v_ref[:, cols].T
        k_tile = k_ref[:, cols]
        for odd in range(2):
            chip, j = divmod(2 * pair + odd, per_chip)
            part = slice(odd * head_size, (odd + 1) * head_size)
            out_ref[chip, j, 0] = q_t[part]
            out_ref[chip, j, 1] = jnp.concatenate([k_tile[:half, part], k_tile[half:, part]], axis=1)
            out_ref[chip, j, 2] = v_t[part]


def pack(queries, keys, values, *, chips, per_chip, head_size):
    tokens, width = queries.shape
    steps = 8
    spec = pl.BlockSpec((tokens, width // steps), lambda i: (0, i))
    return pl.pallas_call(
        functools.partial(pack_kernel, per_chip=per_chip, head_size=head_size),
        grid=(steps,),
        in_specs=[spec] * 3,
        out_specs=pl.BlockSpec(
            (chips // steps, per_chip, 3, head_size, tokens), lambda i: (i, 0, 0, 0, 0)
        ),
        out_shape=jax.ShapeDtypeStruct((chips, per_chip, 3, head_size, tokens), queries.dtype),
        name="pack",
    )(queries, keys, values)


def attend_kernel(slots_ref, counts_ref, mine_ref, other_ref, out_ref, kv, *, scale, list_most):
    blocks, _, _, head_size, tokens = mine_ref.shape
    head = pl.program_id(0)
    for b in range(blocks):
        kv[b] = mine_ref[b, 0, 1:3]
        kv[blocks + b] = other_ref[b, 0]
    entries = 1 + list_most
    ones = jnp.ones((SUM_ROWS, tokens), jnp.bfloat16)
    zeros = jnp.zeros((head_size, tokens), jnp.bfloat16)

    def rows_of(base, counts, seen):
        scores, values = [], []
        for r in range(ROWS):
            row = (head * blocks + base + r) * entries
            own = slots_ref[row]
            q_t = mine_ref[base + r, 0, 0]
            both = [jnp.concatenate([q_t, zeros], axis=1), jnp.concatenate([zeros, q_t], axis=1)]
            keys, vals = [kv[own, 0]], [jnp.concatenate([kv[own, 1], ones], axis=0)]
            for e in range(1, seen):
                live = e <= counts[r]
                slot = jnp.where(live, slots_ref[row + e], own)
                factor = jnp.where(live, 1.0, 0.0).astype(jnp.bfloat16)
                keys.append(kv[slot, 0])
                vals.append(jnp.concatenate([kv[slot, 1], ones], axis=0) * factor)
            scores.append(
                jnp.dot(
                    jnp.concatenate(keys, axis=0),
                    jnp.concatenate(both, axis=0),
                    preferred_element_type=jnp.float32,
                )
            )
            values.append(jnp.concatenate(vals, axis=1))
        for r in range(ROWS):
            top = jnp.max(scores[r], axis=0, keepdims=True)
            top = jnp.maximum(top[:, :tokens], top[:, tokens:])
            top = jnp.concatenate([top, top], axis=1)
            probs = jnp.exp2((scores[r] - top) * scale).astype(jnp.bfloat16)
            probs = [
                probs[e * head_size : (e + 1) * head_size, c * tokens : (c + 1) * tokens]
                for e in range(seen)
                for c in range(2)
            ]
            total = jnp.dot(
                values[r], jnp.concatenate(probs, axis=0), preferred_element_type=jnp.float32
            )
            out_ref[base + r, 0] = (total[:head_size] / total[head_size : head_size + 1]).astype(
                out_ref.dtype
            )

    def group(g, carry):
        base = g * ROWS
        counts = [counts_ref[head * blocks + base + r] for r in range(ROWS)]
        seen = 1 + functools.reduce(jnp.maximum, counts)
        below = 0
        for size in (*range(3, entries, 2), entries):
            pl.when((seen > below) & (seen <= size))(
                functools.partial(rows_of, base, counts, size)
            )
            below = size
        return carry

    lax.fori_loop(0, blocks // ROWS, group, 0)


def attend(slots, counts, mine, other, *, list_most):
    blocks, per_chip, _, head_size, tokens = mine.shape
    return pl.pallas_call(
        functools.partial(
            attend_kernel, scale=LOG2E / math.sqrt(head_size), list_most=list_most
        ),
        grid_spec=pltpu.PrefetchScalarGridSpec(
            num_scalar_prefetch=2,
            grid=(per_chip,),
            in_specs=[
                pl.BlockSpec((blocks, 1, 3, head_size, tokens), lambda j, s, c: (0, j, 0, 0, 0)),
                pl.BlockSpec((blocks, 1, 2, head_size, tokens), lambda j, s, c: (0, j, 0, 0, 0)),
            ],
            out_specs=pl.BlockSpec((blocks, 1, head_size, tokens), lambda j, s, c: (0, j, 0, 0)),
            scratch_shapes=[pltpu.VMEM((2 * blocks, 2, head_size, tokens), jnp.bfloat16)],
        ),
        out_shape=jax.ShapeDtypeStruct((blocks, per_chip, head_size, tokens), mine.dtype),
        compiler_params=pltpu.CompilerParams(vmem_limit_bytes=48 << 20),
        name="attend",
    )(slots, counts, mine, other)


def on_pair(projected, key_lists, list_counts, *, chips_seq, head_count):
    tokens, _, width = projected.shape
    heads_dev, blocks_dev, list_most = key_lists.shape
    chips = chips_seq * head_count
    head_size = width // (heads_dev * head_count)
    per_chip = heads_dev // chips_seq
    core = lax.axis_index("core")

    table = jnp.concatenate([key_lists, list_counts[:, :, None]], axis=2)
    table = lax.all_to_all(
        table.reshape(chips_seq, per_chip, blocks_dev, list_most + 1),
        "chip", split_axis=0, concat_axis=0, tiled=True,
    )
    table = table.transpose(1, 2, 0, 3).reshape(per_chip * chips, list_most + 1)
    listed, counts = table[:, :list_most], table[:, list_most]
    shard = listed // blocks_dev
    slots = (
        ((shard % PAIR) != core).astype(jnp.int32) * chips
        + (listed % blocks_dev) * chips_seq
        + shard // PAIR
    )
    own = jnp.arange(per_chip * chips, dtype=jnp.int32)[:, None] % chips
    slots = jnp.concatenate([own, slots], axis=1).reshape(-1)

    packed = pack(
        projected[:, 0], projected[:, 1], projected[:, 2],
        chips=chips, per_chip=per_chip, head_size=head_size,
    )
    mine = lax.all_to_all(packed, ("head", "chip"), split_axis=0, concat_axis=0, tiled=True)
    other = lax.ppermute(mine[:, :, 1:], "core", [(0, 1), (1, 0)])
    attended = attend(slots, counts, mine, other, list_most=list_most)
    back = lax.all_to_all(attended, ("head", "chip"), split_axis=0, concat_axis=0, tiled=True)
    return back.reshape(width, tokens).T


def attend_rows(query_part, gathered, live_cols, head_size):
    row_count, seen_blocks, block_len, doubled = gathered.shape
    key_rows = gathered[..., :head_size].reshape(row_count, seen_blocks * block_len, head_size)
    value_rows = gathered[..., head_size:].reshape(row_count, seen_blocks * block_len, head_size)
    attention_scores = jnp.einsum(
        "rqd,rkd->rqk", query_part, key_rows, preferred_element_type=jnp.float32
    ) * (1.0 / math.sqrt(head_size))
    attention_scores = attention_scores.reshape(row_count, block_len, seen_blocks, block_len)
    attention_scores = jnp.where(live_cols[:, None, :, None], attention_scores, NEG_FILL)
    row_top = jnp.max(attention_scores, axis=(2, 3), keepdims=True)
    exp_scores = jnp.exp(attention_scores - row_top)
    attention_weights = (exp_scores / jnp.sum(exp_scores, axis=(2, 3), keepdims=True)).astype(
        jnp.bfloat16
    )
    attention_weights = attention_weights.reshape(row_count, block_len, seen_blocks * block_len)
    return jnp.einsum(
        "rqk,rkd->rqd", attention_weights, value_rows, preferred_element_type=jnp.float32
    )


def on_device(projected, key_lists, list_counts):
    seq_count = lax.axis_size("seq")
    heads_dev, blocks_dev, list_most = key_lists.shape
    regrouped = lax.all_to_all(projected, "head", split_axis=2, concat_axis=0, tiled=True)
    block_len = regrouped.shape[0] // blocks_dev
    group_width = regrouped.shape[2]
    head_size = group_width // heads_dev
    row_count = heads_dev * blocks_dev
    splitted = regrouped.reshape(blocks_dev, block_len, 3, heads_dev, head_size)
    queries = splitted[:, :, 0].transpose(2, 0, 1, 3).reshape(row_count, block_len, head_size)
    kv_pairs = jnp.concatenate([splitted[:, :, 1], splitted[:, :, 2]], axis=-1)
    kv_pairs = kv_pairs.transpose(2, 0, 1, 3).reshape(row_count, block_len, 2 * head_size)
    entries = key_lists.reshape(row_count * list_most)
    owners = entries // blocks_dev
    row_head = jnp.arange(row_count * list_most, dtype=jnp.int32) // (blocks_dev * list_most)
    capacity = row_count * list_most // seq_count
    wanted = row_head * blocks_dev + entries % blocks_dev
    onehot = (owners[:, None] == jnp.arange(seq_count, dtype=jnp.int32)[None, :]).astype(jnp.int32)
    within = jnp.sum(onehot * (jnp.cumsum(onehot, axis=0) - 1), axis=1)
    slot_ids = owners * capacity + within
    request = (
        jnp.zeros((seq_count * capacity,), jnp.int32)
        .at[slot_ids]
        .set(wanted)
        .reshape(seq_count, capacity)
    )
    asked_for = lax.all_to_all(request, "seq", split_axis=0, concat_axis=0, tiled=True)
    served = jnp.take(kv_pairs, asked_for.reshape(-1), axis=0).reshape(
        seq_count, capacity, block_len, 2 * head_size
    )
    fetched = lax.all_to_all(served, "seq", split_axis=0, concat_axis=0, tiled=True)
    fetched = fetched.reshape(seq_count * capacity, block_len, 2 * head_size)
    entry_slots = slot_ids.reshape(row_count, list_most)
    row_counts = list_counts.reshape(row_count)
    group_rows = 4

    def one_group(group_index):
        start = group_index * group_rows
        query_part = lax.dynamic_slice_in_dim(queries, start, group_rows, 0)
        own_pairs = lax.dynamic_slice_in_dim(kv_pairs, start, group_rows, 0)
        slot_part = lax.dynamic_slice_in_dim(entry_slots, start, group_rows, 0)
        count_part = lax.dynamic_slice_in_dim(row_counts, start, group_rows, 0)
        listed = jnp.take(fetched, slot_part.reshape(-1), axis=0).reshape(
            group_rows, list_most, block_len, 2 * head_size
        )
        gathered = jnp.concatenate([own_pairs[:, None], listed], axis=1)
        live_cols = jnp.concatenate(
            [
                jnp.ones((group_rows, 1), bool),
                jnp.arange(list_most, dtype=jnp.int32)[None, :] < count_part[:, None],
            ],
            axis=1,
        )
        return attend_rows(query_part, gathered, live_cols, head_size).astype(jnp.bfloat16)

    attended = lax.map(one_group, jnp.arange(row_count // group_rows, dtype=jnp.int32))
    attended = attended.reshape(row_count, block_len, head_size)
    laid_out = attended.reshape(heads_dev, blocks_dev * block_len, head_size).transpose(1, 0, 2)
    laid_out = laid_out.reshape(blocks_dev * block_len, group_width)
    return lax.all_to_all(laid_out, "head", split_axis=0, concat_axis=1, tiled=True)


def whole_heads_fit(mesh, projected, key_lists):
    seq_count, head_count = mesh.shape["seq"], mesh.shape["head"]
    if seq_count % PAIR:
        return False
    chips_seq = seq_count // PAIR
    chips = chips_seq * head_count
    group_heads = key_lists.shape[0] // head_count
    one_block = key_lists.shape[1] == seq_count * head_count
    return one_block and group_heads % chips_seq == 0 and chips % 8 == 0 and chips % ROWS == 0


def solution(mesh):
    seq_count, head_count = mesh.shape["seq"], mesh.shape["head"]

    def run(projected, key_lists, list_counts):
        if not whole_heads_fit(mesh, projected, key_lists):
            return jax.shard_map(
                on_device,
                mesh=mesh,
                in_specs=(P(("seq", "head"), None, None), P("head", "seq", None), P("head", "seq")),
                out_specs=P(("seq", "head"), None),
                check_vma=False,
            )(projected, key_lists, list_counts)
        chips_seq = seq_count // PAIR
        split = Mesh(mesh.devices.reshape(chips_seq, PAIR, head_count), ("chip", "core", "head"))
        seq = ("chip", "core")
        return jax.shard_map(
            functools.partial(on_pair, chips_seq=chips_seq, head_count=head_count),
            mesh=split,
            in_specs=(P(seq + ("head",), None, None), P("head", seq, None), P("head", seq)),
            out_specs=P(seq + ("head",), None),
            check_vma=False,
        )(projected, key_lists, list_counts)

    return run
```

```python
import functools
import math

import jax
import jax.numpy as jnp
from jax import lax
from jax.experimental import pallas as pl
from jax.experimental.pallas import tpu as pltpu
from jax.sharding import Mesh
from jax.sharding import PartitionSpec as P

NEG_FILL = -1e30
LOG2E = 1.4426950408889634
PAIR = 2
ROWS = 8
SUM_ROWS = 16


def head_of(natural, j, chips_seq, per_chip):
    z, p = divmod(natural, chips_seq)
    paired = per_chip // 2 * 2
    group = z * chips_seq * per_chip
    if j < paired:
        return group + p * paired + j
    return group + chips_seq * paired + p


def pack_kernel(
    me_ref, q_ref, k_ref, v_ref, *rest, single, paired, chips_seq, head_count, per_chip
):
    apart, own, joined = rest[:head_count], rest[head_count], rest[head_count + 1 : -2]
    held_one, held = rest[-2:]
    tokens = q_ref.shape[0]
    head_size = held.shape[-2]
    half, lanes = tokens // 2, 2 * head_size
    places = {}
    for natural in range(chips_seq * head_count):
        for to, heads in ((held_one, single), (held, paired)):
            for at, j in enumerate(heads):
                tile, odd = divmod(head_of(natural, j, chips_seq, per_chip), 2)
                places.setdefault(tile, []).append((natural, to, at, odd))
    for tile, users in places.items():
        cols = slice(tile * lanes, (tile + 1) * lanes)
        q_t = q_ref[:, cols].T
        v_t = v_ref[:, cols].T
        k_tile = k_ref[:, cols]
        for natural, to, at, odd in users:
            part = slice(odd * head_size, (odd + 1) * head_size)
            z, p = divmod(natural, chips_seq)
            to = to.at[p, z ^ me_ref[0], at]
            to[0] = jnp.concatenate([k_tile[:half, part], k_tile[half:, part]], axis=1)
            to[1] = v_t[part]
            to[2] = q_t[part]
    for kz in range(head_count):
        apart[kz][...] = held_one[:, kz]
    own[...] = held[:, 0]
    for kp in range(chips_seq):
        joined[kp][...] = held[me_ref[1] ^ kp, 1:]


def pack(me, queries, keys, values, *, chips_seq, head_count, per_chip, head_size):
    tokens, width = queries.shape
    whole = pl.BlockSpec((tokens, width), lambda i, me: (0, 0))
    single, paired = (per_chip - 1,), tuple(range(per_chip - 1))
    part = (3, head_size, tokens)
    shapes = [(chips_seq, 1, *part)] * head_count
    shapes.append((chips_seq, len(paired), *part))
    shapes += [(head_count - 1, len(paired), *part)] * chips_seq
    return pl.pallas_call(
        functools.partial(
            pack_kernel,
            single=single, paired=paired,
            chips_seq=chips_seq, head_count=head_count, per_chip=per_chip,
        ),
        grid_spec=pltpu.PrefetchScalarGridSpec(
            num_scalar_prefetch=1,
            grid=(1,),
            in_specs=[whole] * 3,
            out_specs=[pl.BlockSpec(s, lambda i, me, n=len(s): (0,) * n) for s in shapes],
            scratch_shapes=[
                pltpu.VMEM((chips_seq, head_count, len(heads), *part), queries.dtype)
                for heads in (single, paired)
            ],
        ),
        out_shape=[jax.ShapeDtypeStruct(s, queries.dtype) for s in shapes],
        compiler_params=pltpu.CompilerParams(vmem_limit_bytes=48 << 20),
        name="pack",
    )(me, queries, keys, values)


def attend_kernel(
    me_ref, table_ref, *rest, scale, entries, chips_seq, head_count, per_chip, j, near
):
    mine, other = rest[:head_count], rest[head_count : 2 * head_count]
    out_ref, q, kv = rest[-3:]
    blocks, head_size, tokens = q.shape
    paired = per_chip // 2 * 2
    head = me_ref[1] * paired + j if j < paired else chips_seq * paired + me_ref[1]
    head = head + pl.program_id(0)
    for kz in range(head_count):
        for p in range(chips_seq):
            natural = (me_ref[0] ^ kz) * chips_seq + (p ^ me_ref[1] if near and kz else p)
            q[natural] = mine[kz][p, 0, 2]
            kv[natural] = mine[kz][p, 0, :2]
            kv[blocks + natural] = other[kz][p, 0]
    ones = jnp.ones((SUM_ROWS, tokens), jnp.bfloat16)
    zeros = jnp.zeros((head_size, tokens), jnp.bfloat16)

    def row_of(base, r):
        return r % chips_seq, base // chips_seq + r // chips_seq

    def rows_of(base, counts, seen):
        scores, values = [], []
        for r in range(ROWS):
            p, z = row_of(base, r)
            own = base + r
            q_t = q[own]
            both = [jnp.concatenate([q_t, zeros], axis=1), jnp.concatenate([zeros, q_t], axis=1)]
            keys, vals = [kv[own, 0]], [jnp.concatenate([kv[own, 1], ones], axis=0)]
            for e in range(1, seen):
                live = e <= counts[r]
                slot = jnp.where(live, table_ref[p, head, z, e - 1], own)
                factor = jnp.where(live, 1.0, 0.0).astype(jnp.bfloat16)
                keys.append(kv[slot, 0])
                vals.append(jnp.concatenate([kv[slot, 1], ones], axis=0) * factor)
            scores.append(
                jnp.dot(
                    jnp.concatenate(keys, axis=0),
                    jnp.concatenate(both, axis=0),
                    preferred_element_type=jnp.float32,
                )
            )
            values.append(jnp.concatenate(vals, axis=1))
        for r in range(ROWS):
            top = jnp.max(scores[r], axis=0, keepdims=True)
            top = jnp.maximum(top[:, :tokens], top[:, tokens:])
            top = jnp.concatenate([top, top], axis=1)
            probs = jnp.exp2((scores[r] - top) * scale).astype(jnp.bfloat16)
            probs = [
                probs[e * head_size : (e + 1) * head_size, c * tokens : (c + 1) * tokens]
                for e in range(seen)
                for c in range(2)
            ]
            total = jnp.dot(
                values[r], jnp.concatenate(probs, axis=0), preferred_element_type=jnp.float32
            )
            out_ref[base + r, 0] = (total[:head_size] / total[head_size : head_size + 1]).astype(
                out_ref.dtype
            )

    def group(g, carry):
        base = g * ROWS
        counts = []
        for r in range(ROWS):
            p, z = row_of(base, r)
            counts.append(table_ref[p, head, z, entries - 1])
        seen = 1 + functools.reduce(jnp.maximum, counts)
        below = 0
        for size in (*range(3, entries, 2), entries):
            pl.when((seen > below) & (seen <= size))(
                functools.partial(rows_of, base, counts, size)
            )
            below = size
        return carry

    lax.fori_loop(0, blocks // ROWS, group, 0)


def attend(
    me, table, mine, other, held, *, entries, j, near, per_chip, chips_seq, head_count
):
    blocks = chips_seq * head_count
    block = mine[0][0].shape[-2:]
    head_size, tokens = block

    def spec(at, parts):
        return pl.BlockSpec((chips_seq, 1, parts, *block), lambda i, *_: (0, at + i, 0, 0, 0))

    in_specs = [spec(at, 3) for _, at in mine] + [spec(at, 2) for _, at in other]
    operands = [me, table] + [array for array, _ in mine + other]
    dtype = mine[0][0].dtype
    aliases = {}
    if held is not None:
        in_specs.append(pl.BlockSpec(memory_space=pl.ANY))
        aliases = {len(operands): 0}
        operands.append(held)
    return pl.pallas_call(
        functools.partial(
            attend_kernel,
            scale=LOG2E / math.sqrt(head_size), entries=entries,
            chips_seq=chips_seq, head_count=head_count, per_chip=per_chip, j=j, near=near,
        ),
        grid_spec=pltpu.PrefetchScalarGridSpec(
            num_scalar_prefetch=2,
            grid=(mine[-1][0].shape[1] - mine[-1][1],) if near else (1,),
            in_specs=in_specs,
            out_specs=pl.BlockSpec((blocks, 1, *block), lambda i, *_: (0, j + i, 0, 0)),
            scratch_shapes=[
                pltpu.VMEM((blocks, *block), dtype),
                pltpu.VMEM((2 * blocks, 2, *block), dtype),
            ],
        ),
        out_shape=jax.ShapeDtypeStruct((blocks, per_chip, *block), dtype),
        input_output_aliases=aliases,
        compiler_params=pltpu.CompilerParams(vmem_limit_bytes=48 << 20),
        cost_estimate=pl.CostEstimate(flops=1, transcendentals=1, bytes_accessed=1),
        name="attend",
    )(*operands)


def sync(*values):
    return lax.optimization_barrier(values)


def swap(value, axis, k):
    size = lax.axis_size(axis)
    return lax.ppermute(value, axis, [(i, i ^ k) for i in range(size)])


def on_pair(projected, key_lists, list_counts, *, chips_seq, head_count):
    tokens, _, width = projected.shape
    heads_dev, blocks_dev, list_most = key_lists.shape
    chips = chips_seq * head_count
    head_size = width // (heads_dev * head_count)
    per_chip = heads_dev // chips_seq
    entries = 1 + list_most
    core = lax.axis_index("core")
    me = jnp.stack([lax.axis_index("head"), lax.axis_index("chip")]).astype(jnp.int32)

    shard = key_lists // blocks_dev
    slots = (
        ((shard % PAIR) != core).astype(jnp.int32) * chips
        + (key_lists % blocks_dev) * chips_seq
        + shard // PAIR
    )
    table = jnp.concatenate([slots, list_counts[:, :, None]], axis=2)

    qkv = projected[:, 0], projected[:, 1], projected[:, 2]
    sizes = dict(chips_seq=chips_seq, head_count=head_count, per_chip=per_chip)

    def over(parts, axis, name):
        with jax.named_scope(name):
            return [parts[0]] + [swap(parts[k], axis, k) for k in range(1, len(parts))]

    def over_p(value, name):
        with jax.named_scope(name):
            return lax.all_to_all(value, "chip", split_axis=0, concat_axis=0, tiled=True)

    def over_cores(value, name):
        with jax.named_scope(name):
            return swap(value, "core", 1)

    def heads(c, mine, other, held, table, near):
        with jax.named_scope(f"heads{c}"):
            return attend(me, table, mine, other, held, entries=entries, j=c, near=near, **sizes)

    last, each = per_chip - 1, range(head_count)
    packed = pack(me, *qkv, head_size=head_size, **sizes)
    packed, table = sync(packed, table)
    singles, own, pairs = packed[:head_count], packed[head_count], packed[head_count + 1 :]
    seen = list_counts[0, 0] > 0

    def last_head(singles, own, table):
        plane = over_p(jnp.concatenate([jnp.stack(singles, axis=1)[:, :, 0], own], axis=1), "plane")
        other = over_cores(plane, "cores2")
        held = heads(
            last, [(plane, kz) for kz in each], [(other, kz) for kz in each], None, table, False
        )
        return plane, other, held

    def none(*operands):
        shapes = jax.eval_shape(last_head, *operands)
        return jax.tree.map(lambda s: jnp.zeros(s.shape, s.dtype), shapes)

    pairs = over(pairs, "chip", "p01")
    singles = over(singles, "head", "z2")
    table = over_p(jnp.broadcast_to(table[None], (chips_seq, *table.shape)), "lists")
    singles, pairs, table = sync(singles, pairs, table)
    with jax.named_scope("z01"):
        rest = [
            swap(jnp.stack([part[k - 1] for part in pairs]), "head", k)
            for k in range(1, head_count)
        ]
    plane, other, held = lax.cond(seen, last_head, none, singles, own, table)
    rest, held = sync(rest, held)
    mine = [(plane, head_count)] + [(part, 0) for part in rest]
    other = [(other, head_count)] + [(over_cores(part, "cores01"), 0) for part in rest]
    held = heads(0, mine, other, held, table, True)
    back = lax.all_to_all(held, ("head", "chip"), split_axis=0, concat_axis=0, tiled=True)
    back = back.reshape(head_count, chips_seq, per_chip, head_size, tokens)
    paired = per_chip // 2 * 2
    back = jnp.concatenate(
        [
            back[:, :, :paired].reshape(head_count, chips_seq * paired, head_size, tokens),
            back[:, :, paired:].reshape(head_count, -1, head_size, tokens),
        ],
        axis=1,
    )
    return back.reshape(width, tokens).T


def attend_rows(query_part, gathered, live_cols, head_size):
    row_count, seen_blocks, block_len, doubled = gathered.shape
    key_rows = gathered[..., :head_size].reshape(row_count, seen_blocks * block_len, head_size)
    value_rows = gathered[..., head_size:].reshape(row_count, seen_blocks * block_len, head_size)
    attention_scores = jnp.einsum(
        "rqd,rkd->rqk", query_part, key_rows, preferred_element_type=jnp.float32
    ) * (1.0 / math.sqrt(head_size))
    attention_scores = attention_scores.reshape(row_count, block_len, seen_blocks, block_len)
    attention_scores = jnp.where(live_cols[:, None, :, None], attention_scores, NEG_FILL)
    row_top = jnp.max(attention_scores, axis=(2, 3), keepdims=True)
    exp_scores = jnp.exp(attention_scores - row_top)
    attention_weights = (exp_scores / jnp.sum(exp_scores, axis=(2, 3), keepdims=True)).astype(
        jnp.bfloat16
    )
    attention_weights = attention_weights.reshape(row_count, block_len, seen_blocks * block_len)
    return jnp.einsum(
        "rqk,rkd->rqd", attention_weights, value_rows, preferred_element_type=jnp.float32
    )


def on_device(projected, key_lists, list_counts):
    seq_count = lax.axis_size("seq")
    heads_dev, blocks_dev, list_most = key_lists.shape
    regrouped = lax.all_to_all(projected, "head", split_axis=2, concat_axis=0, tiled=True)
    block_len = regrouped.shape[0] // blocks_dev
    group_width = regrouped.shape[2]
    head_size = group_width // heads_dev
    row_count = heads_dev * blocks_dev
    splitted = regrouped.reshape(blocks_dev, block_len, 3, heads_dev, head_size)
    queries = splitted[:, :, 0].transpose(2, 0, 1, 3).reshape(row_count, block_len, head_size)
    kv_pairs = jnp.concatenate([splitted[:, :, 1], splitted[:, :, 2]], axis=-1)
    kv_pairs = kv_pairs.transpose(2, 0, 1, 3).reshape(row_count, block_len, 2 * head_size)
    entries = key_lists.reshape(row_count * list_most)
    owners = entries // blocks_dev
    row_head = jnp.arange(row_count * list_most, dtype=jnp.int32) // (blocks_dev * list_most)
    capacity = row_count * list_most // seq_count
    wanted = row_head * blocks_dev + entries % blocks_dev
    onehot = (owners[:, None] == jnp.arange(seq_count, dtype=jnp.int32)[None, :]).astype(jnp.int32)
    within = jnp.sum(onehot * (jnp.cumsum(onehot, axis=0) - 1), axis=1)
    slot_ids = owners * capacity + within
    request = (
        jnp.zeros((seq_count * capacity,), jnp.int32)
        .at[slot_ids]
        .set(wanted)
        .reshape(seq_count, capacity)
    )
    asked_for = lax.all_to_all(request, "seq", split_axis=0, concat_axis=0, tiled=True)
    served = jnp.take(kv_pairs, asked_for.reshape(-1), axis=0).reshape(
        seq_count, capacity, block_len, 2 * head_size
    )
    fetched = lax.all_to_all(served, "seq", split_axis=0, concat_axis=0, tiled=True)
    fetched = fetched.reshape(seq_count * capacity, block_len, 2 * head_size)
    entry_slots = slot_ids.reshape(row_count, list_most)
    row_counts = list_counts.reshape(row_count)
    group_rows = 4

    def one_group(group_index):
        start = group_index * group_rows
        query_part = lax.dynamic_slice_in_dim(queries, start, group_rows, 0)
        own_pairs = lax.dynamic_slice_in_dim(kv_pairs, start, group_rows, 0)
        slot_part = lax.dynamic_slice_in_dim(entry_slots, start, group_rows, 0)
        count_part = lax.dynamic_slice_in_dim(row_counts, start, group_rows, 0)
        listed = jnp.take(fetched, slot_part.reshape(-1), axis=0).reshape(
            group_rows, list_most, block_len, 2 * head_size
        )
        gathered = jnp.concatenate([own_pairs[:, None], listed], axis=1)
        live_cols = jnp.concatenate(
            [
                jnp.ones((group_rows, 1), bool),
                jnp.arange(list_most, dtype=jnp.int32)[None, :] < count_part[:, None],
            ],
            axis=1,
        )
        return attend_rows(query_part, gathered, live_cols, head_size).astype(jnp.bfloat16)

    attended = lax.map(one_group, jnp.arange(row_count // group_rows, dtype=jnp.int32))
    attended = attended.reshape(row_count, block_len, head_size)
    laid_out = attended.reshape(heads_dev, blocks_dev * block_len, head_size).transpose(1, 0, 2)
    laid_out = laid_out.reshape(blocks_dev * block_len, group_width)
    return lax.all_to_all(laid_out, "head", split_axis=0, concat_axis=1, tiled=True)


def whole_heads_fit(mesh, projected, key_lists):
    seq_count, head_count = mesh.shape["seq"], mesh.shape["head"]
    if seq_count % PAIR:
        return False
    chips_seq = seq_count // PAIR
    chips = chips_seq * head_count
    group_heads = key_lists.shape[0] // head_count
    one_block = key_lists.shape[1] == seq_count * head_count
    powers = all(n & (n - 1) == 0 for n in (chips_seq, head_count))
    if not (one_block and powers and group_heads % chips_seq == 0 and chips % ROWS == 0):
        return False
    return (group_heads // chips_seq) % 2 == 1 and chips_seq % 2 == 0 and ROWS % chips_seq == 0


def solution(mesh):
    seq_count, head_count = mesh.shape["seq"], mesh.shape["head"]

    def run(projected, key_lists, list_counts):
        if not whole_heads_fit(mesh, projected, key_lists):
            return jax.shard_map(
                on_device,
                mesh=mesh,
                in_specs=(P(("seq", "head"), None, None), P("head", "seq", None), P("head", "seq")),
                out_specs=P(("seq", "head"), None),
                check_vma=False,
            )(projected, key_lists, list_counts)
        chips_seq = seq_count // PAIR
        split = Mesh(mesh.devices.reshape(chips_seq, PAIR, head_count), ("chip", "core", "head"))
        seq = ("chip", "core")
        return jax.shard_map(
            functools.partial(on_pair, chips_seq=chips_seq, head_count=head_count),
            mesh=split,
            in_specs=(P(seq + ("head",), None, None), P("head", seq, None), P("head", seq)),
            out_specs=P(seq + ("head",), None),
            check_vma=False,
        )(projected, key_lists, list_counts)

    return run
```

```python
import functools
import math

import jax
import jax.numpy as jnp
from jax import lax
from jax.experimental import pallas as pl
from jax.experimental.pallas import tpu as pltpu
from jax.sharding import Mesh
from jax.sharding import PartitionSpec as P

NEG_FILL = -1e30
LOG2E = 1.4426950408889634
PAIR = 2
ROWS = 8
SUM_ROWS = 16


def head_of(natural, j, chips_seq, per_chip):
    z, p = divmod(natural, chips_seq)
    paired = per_chip // 2 * 2
    group = z * chips_seq * per_chip
    if j < paired:
        return group + p * paired + j
    return group + chips_seq * paired + p


def pack_kernel(
    me_ref, q_ref, k_ref, v_ref, lists_ref, used_ref, *rest,
    single, paired, chips_seq, head_count, per_chip
):
    apart, own, joined = rest[:head_count], rest[head_count], rest[head_count + 1 : -3]
    held_one, held, table = rest[-3:]
    table[...] = jnp.zeros_like(table)
    tokens = q_ref.shape[0]
    head_size = held.shape[-2]
    half, lanes = tokens // 2, 2 * head_size
    places = {}
    for natural in range(chips_seq * head_count):
        for to, heads in ((held_one, single), (held, paired)):
            for at, j in enumerate(heads):
                tile, odd = divmod(head_of(natural, j, chips_seq, per_chip), 2)
                places.setdefault(tile, []).append((natural, to, at, odd))
    for tile, users in places.items():
        cols = slice(tile * lanes, (tile + 1) * lanes)
        q_t = q_ref[:, cols].T
        v_t = v_ref[:, cols].T
        k_tile = k_ref[:, cols]
        for natural, to, at, odd in users:
            part = slice(odd * head_size, (odd + 1) * head_size)
            z, p = divmod(natural, chips_seq)
            to = to.at[p, z ^ me_ref[0], at]
            to[0] = jnp.concatenate([k_tile[:half, part], k_tile[half:, part]], axis=1)
            to[1] = v_t[part]
            to[2] = q_t[part]
    for kz in range(head_count):
        apart[-1 - kz][...] = held_one[:, kz]
    own[...] = held[:, 0]
    for kp in range(chips_seq):
        p, many = me_ref[1] ^ kp, len(paired)
        for at, head in enumerate([p * many + j for j in paired] + [chips_seq * many + p]):
            listed = lists_ref[head]
            shard = listed // head_count
            slots = (shard % PAIR != me_ref[2]).astype(jnp.int32) * (chips_seq * head_count)
            slots += listed % head_count * chips_seq + shard // PAIR
            table[at * head_count : (at + 1) * head_count, : listed.shape[1]] = slots.astype(
                jnp.float32
            )
            table[pl.ds(per_chip * head_count + at, 1), :head_count] = used_ref[
                pl.ds(head, 1)
            ].astype(jnp.float32)
        lists = table[...].astype(joined[kp].dtype)
        rows = joined[kp].shape[0] - lists.shape[0]
        joined[kp][:rows] = held[me_ref[1] ^ kp, 1:].reshape(rows, tokens)
        joined[kp][rows:] = lists


def list_rows(per_chip, head_count):
    return pl.cdiv(per_chip * (head_count + 1), 16) * 16


def pack(me, queries, keys, values, lists, used, *, chips_seq, head_count, per_chip, head_size):
    tokens, width = queries.shape
    whole = pl.BlockSpec((tokens, width), lambda i, me: (0, 0))
    single, paired = (per_chip - 1,), tuple(range(per_chip - 1))
    part = (3, head_size, tokens)
    shapes = [(chips_seq, 1, *part)] * head_count
    shapes.append((chips_seq, len(paired), *part))
    rows = (head_count - 1) * len(paired) * math.prod(part[:-1]) + list_rows(per_chip, head_count)
    shapes += [(rows, tokens)] * chips_seq
    return pl.pallas_call(
        functools.partial(
            pack_kernel,
            single=single, paired=paired,
            chips_seq=chips_seq, head_count=head_count, per_chip=per_chip,
        ),
        grid_spec=pltpu.PrefetchScalarGridSpec(
            num_scalar_prefetch=1,
            grid=(1,),
            in_specs=[
                *[whole] * 3,
                pl.BlockSpec(lists.shape, lambda i, me: (0, 0, 0)),
                pl.BlockSpec(used.shape, lambda i, me: (0, 0)),
            ],
            out_specs=[pl.BlockSpec(s, lambda i, me, n=len(s): (0,) * n) for s in shapes],
            scratch_shapes=[
                pltpu.VMEM((chips_seq, head_count, len(heads), *part), queries.dtype)
                for heads in (single, paired)
            ]
            + [pltpu.VMEM((list_rows(per_chip, head_count), tokens), jnp.float32)],
        ),
        out_shape=[jax.ShapeDtypeStruct(s, queries.dtype) for s in shapes],
        compiler_params=pltpu.CompilerParams(vmem_limit_bytes=48 << 20),
        name="pack",
    )(me, queries, keys, values, lists, used)


def attend_kernel(
    me_ref, table_ref, *rest, scale, entries, chips_seq, head_count, per_chip, j, near
):
    mine, other = rest[:head_count], rest[head_count : 2 * head_count]
    out_ref, q, kv = rest[-3:]
    blocks, head_size, tokens = q.shape
    head = j + pl.program_id(0)
    counted = per_chip * head_count + head
    head = head * head_count
    for kz in range(head_count):
        for p in range(chips_seq):
            natural = (me_ref[0] ^ kz) * chips_seq + (p ^ me_ref[1] if near and kz else p)
            q[natural] = mine[kz][p, 0, 2]
            kv[natural] = mine[kz][p, 0, :2]
            kv[blocks + natural] = other[kz][p, 0]
    ones = jnp.ones((SUM_ROWS, tokens), jnp.bfloat16)
    zeros = jnp.zeros((head_size, tokens), jnp.bfloat16)

    def row_of(base, r):
        return r % chips_seq ^ me_ref[1], base // chips_seq + r // chips_seq

    def rows_of(base, counts, seen):
        scores, values = [], []
        for r in range(ROWS):
            p, z = row_of(base, r)
            own = base + r
            q_t = q[own]
            both = [jnp.concatenate([q_t, zeros], axis=1), jnp.concatenate([zeros, q_t], axis=1)]
            keys, vals = [kv[own, 0]], [jnp.concatenate([kv[own, 1], ones], axis=0)]
            for e in range(1, seen):
                live = e <= counts[r]
                slot = jnp.where(live, table_ref[p, head + z, e - 1], own)
                factor = jnp.where(live, 1.0, 0.0).astype(jnp.bfloat16)
                keys.append(kv[slot, 0])
                vals.append(jnp.concatenate([kv[slot, 1], ones], axis=0) * factor)
            scores.append(
                jnp.dot(
                    jnp.concatenate(keys, axis=0),
                    jnp.concatenate(both, axis=0),
                    preferred_element_type=jnp.float32,
                )
            )
            values.append(jnp.concatenate(vals, axis=1))
        for r in range(ROWS):
            top = jnp.max(scores[r], axis=0, keepdims=True)
            top = jnp.maximum(top[:, :tokens], top[:, tokens:])
            top = jnp.concatenate([top, top], axis=1)
            probs = jnp.exp2((scores[r] - top) * scale).astype(jnp.bfloat16)
            probs = [
                probs[e * head_size : (e + 1) * head_size, c * tokens : (c + 1) * tokens]
                for e in range(seen)
                for c in range(2)
            ]
            total = jnp.dot(
                values[r], jnp.concatenate(probs, axis=0), preferred_element_type=jnp.float32
            )
            out_ref[base + r, 0] = (total[:head_size] / total[head_size : head_size + 1]).astype(
                out_ref.dtype
            )

    def group(g, carry):
        base = g * ROWS
        counts = []
        for r in range(ROWS):
            p, z = row_of(base, r)
            counts.append(table_ref[p, counted, z])
        seen = 1 + functools.reduce(jnp.maximum, counts)
        below = 0
        for size in (*range(3, entries, 2), entries):
            pl.when((seen > below) & (seen <= size))(
                functools.partial(rows_of, base, counts, size)
            )
            below = size
        return carry

    lax.fori_loop(0, blocks // ROWS, group, 0)


def attend(
    me, table, mine, other, held, *, entries, j, near, per_chip, chips_seq, head_count
):
    blocks = chips_seq * head_count
    block = mine[0][0].shape[-2:]
    head_size, tokens = block

    def spec(at, parts):
        return pl.BlockSpec((chips_seq, 1, parts, *block), lambda i, *_: (0, at + i, 0, 0, 0))

    in_specs = [spec(at, 3) for _, at in mine] + [spec(at, 2) for _, at in other]
    operands = [me, table] + [array for array, _ in mine + other]
    dtype = mine[0][0].dtype
    aliases = {}
    if held is not None:
        in_specs.append(pl.BlockSpec(memory_space=pl.ANY))
        aliases = {len(operands): 0}
        operands.append(held)
    return pl.pallas_call(
        functools.partial(
            attend_kernel,
            scale=LOG2E / math.sqrt(head_size), entries=entries,
            chips_seq=chips_seq, head_count=head_count, per_chip=per_chip, j=j, near=near,
        ),
        grid_spec=pltpu.PrefetchScalarGridSpec(
            num_scalar_prefetch=2,
            grid=(mine[-1][0].shape[1] - mine[-1][1],) if near else (1,),
            in_specs=in_specs,
            out_specs=pl.BlockSpec((blocks, 1, *block), lambda i, *_: (0, j + i, 0, 0)),
            scratch_shapes=[
                pltpu.VMEM((blocks, *block), dtype),
                pltpu.VMEM((2 * blocks, 2, *block), dtype),
            ],
        ),
        out_shape=jax.ShapeDtypeStruct((blocks, per_chip, *block), dtype),
        input_output_aliases=aliases,
        compiler_params=pltpu.CompilerParams(vmem_limit_bytes=48 << 20),
        cost_estimate=pl.CostEstimate(flops=1, transcendentals=1, bytes_accessed=1),
        name="attend",
    )(*operands)


def sync(*values):
    return lax.optimization_barrier(values)


def swap(value, axis, k):
    size = lax.axis_size(axis)
    return lax.ppermute(value, axis, [(i, i ^ k) for i in range(size)])


def on_pair(projected, key_lists, list_counts, *, chips_seq, head_count):
    tokens, _, width = projected.shape
    heads_dev, blocks_dev, list_most = key_lists.shape
    head_size = width // (heads_dev * head_count)
    per_chip = heads_dev // chips_seq
    entries = 1 + list_most
    me = jnp.stack([lax.axis_index(a) for a in ("head", "chip", "core")]).astype(jnp.int32)

    qkv = projected[:, 0], projected[:, 1], projected[:, 2]
    sizes = dict(chips_seq=chips_seq, head_count=head_count, per_chip=per_chip)

    def over(parts, axis, name):
        with jax.named_scope(name):
            return [parts[0]] + [swap(parts[k], axis, k) for k in reversed(range(1, len(parts)))][::-1]

    def over_p(value, name):
        with jax.named_scope(name):
            return lax.all_to_all(value, "chip", split_axis=0, concat_axis=0, tiled=True)

    def over_cores(value, name):
        with jax.named_scope(name):
            return swap(value, "core", 1)

    def heads(c, mine, other, held, table, near):
        with jax.named_scope(f"heads{c}"):
            return attend(me, table, mine, other, held, entries=entries, j=c, near=near, **sizes)

    last, each = per_chip - 1, range(head_count)
    packed = pack(me, *qkv, key_lists, list_counts, head_size=head_size, **sizes)
    singles, own, pairs = packed[head_count - 1 :: -1], packed[head_count], packed[head_count + 1 :]
    seen = list_counts[0, 0] > 0

    def last_head(singles, own, table):
        plane = over_p(jnp.concatenate([jnp.stack(singles, axis=1)[:, :, 0], own], axis=1), "plane")
        other = over_cores(plane, "cores2")
        held = heads(
            last, [(plane, kz) for kz in each], [(other, kz) for kz in each], None, table, False
        )
        return plane, other, held

    def none(*operands):
        shapes = jax.eval_shape(last_head, *operands)
        return jax.tree.map(lambda s: jnp.zeros(s.shape, s.dtype), shapes)

    pairs = over(pairs, "chip", "p01")
    singles = over(singles, "head", "z2")
    rows = pairs[0].shape[0] - list_rows(per_chip, head_count)
    table = jnp.stack([part[rows:, :entries] for part in pairs]).astype(jnp.int32)
    shape = (head_count - 1, per_chip - 1, 3, head_size, tokens)
    pairs = [part[:rows].reshape(shape) for part in pairs]
    with jax.named_scope("z01"):
        rest_sent = [
            jnp.stack([part[k - 1] for part in pairs]) for k in reversed(range(1, head_count))
        ][::-1]
        rest = [swap(rest_sent[k - 1], "head", k) for k in reversed(range(1, head_count))][::-1]
    singles = sync(singles, rest_sent)[0]
    plane, other, held = lax.cond(seen, last_head, none, singles, own, table)
    rest = [sync(part, held)[0] for part in rest]
    mine = [(plane, head_count)] + [(part, 0) for part in rest]
    other = [(other, head_count)] + [(over_cores(part, "cores01"), 0) for part in rest]
    held = heads(0, mine, other, held, table, True)
    back = lax.all_to_all(held, ("head", "chip"), split_axis=0, concat_axis=0, tiled=True)
    back = back.reshape(head_count, chips_seq, per_chip, head_size, tokens)
    paired = per_chip // 2 * 2
    back = jnp.concatenate(
        [
            back[:, :, :paired].reshape(head_count, chips_seq * paired, head_size, tokens),
            back[:, :, paired:].reshape(head_count, -1, head_size, tokens),
        ],
        axis=1,
    )
    return back.reshape(width, tokens).T


def attend_rows(query_part, gathered, live_cols, head_size):
    row_count, seen_blocks, block_len, doubled = gathered.shape
    key_rows = gathered[..., :head_size].reshape(row_count, seen_blocks * block_len, head_size)
    value_rows = gathered[..., head_size:].reshape(row_count, seen_blocks * block_len, head_size)
    attention_scores = jnp.einsum(
        "rqd,rkd->rqk", query_part, key_rows, preferred_element_type=jnp.float32
    ) * (1.0 / math.sqrt(head_size))
    attention_scores = attention_scores.reshape(row_count, block_len, seen_blocks, block_len)
    attention_scores = jnp.where(live_cols[:, None, :, None], attention_scores, NEG_FILL)
    row_top = jnp.max(attention_scores, axis=(2, 3), keepdims=True)
    exp_scores = jnp.exp(attention_scores - row_top)
    attention_weights = (exp_scores / jnp.sum(exp_scores, axis=(2, 3), keepdims=True)).astype(
        jnp.bfloat16
    )
    attention_weights = attention_weights.reshape(row_count, block_len, seen_blocks * block_len)
    return jnp.einsum(
        "rqk,rkd->rqd", attention_weights, value_rows, preferred_element_type=jnp.float32
    )


def on_device(projected, key_lists, list_counts):
    seq_count = lax.axis_size("seq")
    heads_dev, blocks_dev, list_most = key_lists.shape
    regrouped = lax.all_to_all(projected, "head", split_axis=2, concat_axis=0, tiled=True)
    block_len = regrouped.shape[0] // blocks_dev
    group_width = regrouped.shape[2]
    head_size = group_width // heads_dev
    row_count = heads_dev * blocks_dev
    splitted = regrouped.reshape(blocks_dev, block_len, 3, heads_dev, head_size)
    queries = splitted[:, :, 0].transpose(2, 0, 1, 3).reshape(row_count, block_len, head_size)
    kv_pairs = jnp.concatenate([splitted[:, :, 1], splitted[:, :, 2]], axis=-1)
    kv_pairs = kv_pairs.transpose(2, 0, 1, 3).reshape(row_count, block_len, 2 * head_size)
    entries = key_lists.reshape(row_count * list_most)
    owners = entries // blocks_dev
    row_head = jnp.arange(row_count * list_most, dtype=jnp.int32) // (blocks_dev * list_most)
    capacity = row_count * list_most // seq_count
    wanted = row_head * blocks_dev + entries % blocks_dev
    onehot = (owners[:, None] == jnp.arange(seq_count, dtype=jnp.int32)[None, :]).astype(jnp.int32)
    within = jnp.sum(onehot * (jnp.cumsum(onehot, axis=0) - 1), axis=1)
    slot_ids = owners * capacity + within
    request = (
        jnp.zeros((seq_count * capacity,), jnp.int32)
        .at[slot_ids]
        .set(wanted)
        .reshape(seq_count, capacity)
    )
    asked_for = lax.all_to_all(request, "seq", split_axis=0, concat_axis=0, tiled=True)
    served = jnp.take(kv_pairs, asked_for.reshape(-1), axis=0).reshape(
        seq_count, capacity, block_len, 2 * head_size
    )
    fetched = lax.all_to_all(served, "seq", split_axis=0, concat_axis=0, tiled=True)
    fetched = fetched.reshape(seq_count * capacity, block_len, 2 * head_size)
    entry_slots = slot_ids.reshape(row_count, list_most)
    row_counts = list_counts.reshape(row_count)
    group_rows = 4

    def one_group(group_index):
        start = group_index * group_rows
        query_part = lax.dynamic_slice_in_dim(queries, start, group_rows, 0)
        own_pairs = lax.dynamic_slice_in_dim(kv_pairs, start, group_rows, 0)
        slot_part = lax.dynamic_slice_in_dim(entry_slots, start, group_rows, 0)
        count_part = lax.dynamic_slice_in_dim(row_counts, start, group_rows, 0)
        listed = jnp.take(fetched, slot_part.reshape(-1), axis=0).reshape(
            group_rows, list_most, block_len, 2 * head_size
        )
        gathered = jnp.concatenate([own_pairs[:, None], listed], axis=1)
        live_cols = jnp.concatenate(
            [
                jnp.ones((group_rows, 1), bool),
                jnp.arange(list_most, dtype=jnp.int32)[None, :] < count_part[:, None],
            ],
            axis=1,
        )
        return attend_rows(query_part, gathered, live_cols, head_size).astype(jnp.bfloat16)

    attended = lax.map(one_group, jnp.arange(row_count // group_rows, dtype=jnp.int32))
    attended = attended.reshape(row_count, block_len, head_size)
    laid_out = attended.reshape(heads_dev, blocks_dev * block_len, head_size).transpose(1, 0, 2)
    laid_out = laid_out.reshape(blocks_dev * block_len, group_width)
    return lax.all_to_all(laid_out, "head", split_axis=0, concat_axis=1, tiled=True)


def whole_heads_fit(mesh, projected, key_lists):
    seq_count, head_count = mesh.shape["seq"], mesh.shape["head"]
    if seq_count % PAIR:
        return False
    chips_seq = seq_count // PAIR
    chips = chips_seq * head_count
    group_heads = key_lists.shape[0] // head_count
    one_block = key_lists.shape[1] == seq_count * head_count
    powers = all(n & (n - 1) == 0 for n in (chips_seq, head_count))
    if not (one_block and powers and group_heads % chips_seq == 0 and chips % ROWS == 0):
        return False
    small = max(PAIR * chips, key_lists.shape[2]) <= 256
    odd = (group_heads // chips_seq) % 2 == 1
    return small and odd and chips_seq % 2 == 0 and ROWS % chips_seq == 0


def solution(mesh):
    seq_count, head_count = mesh.shape["seq"], mesh.shape["head"]

    def run(projected, key_lists, list_counts):
        if not whole_heads_fit(mesh, projected, key_lists):
            return jax.shard_map(
                on_device,
                mesh=mesh,
                in_specs=(P(("seq", "head"), None, None), P("head", "seq", None), P("head", "seq")),
                out_specs=P(("seq", "head"), None),
                check_vma=False,
            )(projected, key_lists, list_counts)
        chips_seq = seq_count // PAIR
        split = Mesh(mesh.devices.reshape(chips_seq, PAIR, head_count), ("chip", "core", "head"))
        seq = ("chip", "core")
        return jax.shard_map(
            functools.partial(on_pair, chips_seq=chips_seq, head_count=head_count),
            mesh=split,
            in_specs=(P(seq + ("head",), None, None), P("head", seq, None), P("head", seq)),
            out_specs=P(seq + ("head",), None),
            check_vma=False,
        )(projected, key_lists, list_counts)

    return run
```

```python
import functools
import math

import jax
import jax.numpy as jnp
from jax import lax
from jax.experimental import pallas as pl
from jax.experimental.pallas import tpu as pltpu
from jax.sharding import Mesh
from jax.sharding import PartitionSpec as P

NEG_FILL = -1e30
LOG2E = 1.4426950408889634
PAIR = 2
ROWS = 8
SUM_ROWS = 16


def head_of(natural, j, chips_seq, per_chip):
    z, p = divmod(natural, chips_seq)
    paired = per_chip // 2 * 2
    group = z * chips_seq * per_chip
    if j < paired:
        return group + p * paired + j
    return group + chips_seq * paired + p


def pack_kernel(
    me_ref, q_ref, k_ref, v_ref, lists_ref, used_ref, *rest,
    single, paired, chips_seq, head_count, per_chip
):
    apart, own, joined = rest[:head_count], rest[head_count], rest[head_count + 1 : -3]
    held_one, held, table = rest[-3:]
    blocks, list_most, heads = lists_ref.shape
    table[...] = jnp.zeros_like(table)
    for b in range(blocks):
        listed = lists_ref[b]
        shard = listed // head_count
        slots = (shard % PAIR != me_ref[2]).astype(jnp.int32) * (chips_seq * head_count)
        slots += listed % head_count * chips_seq + shard // PAIR
        table[b * list_most : (b + 1) * list_most, :heads] = slots.astype(jnp.float32)
    table[blocks * list_most : blocks * (list_most + 1), :heads] = used_ref[...].astype(jnp.float32)
    lists = table[...].T[: list_rows(heads)].astype(joined[0].dtype)
    tokens = q_ref.shape[0]
    head_size = held.shape[-2]
    half, lanes = tokens // 2, 2 * head_size
    places = {}
    for natural in range(chips_seq * head_count):
        for to, heads in ((held_one, single), (held, paired)):
            for at, j in enumerate(heads):
                tile, odd = divmod(head_of(natural, j, chips_seq, per_chip), 2)
                places.setdefault(tile, []).append((natural, to, at, odd))
    for tile, users in places.items():
        cols = slice(tile * lanes, (tile + 1) * lanes)
        q_t = q_ref[:, cols].T
        v_t = v_ref[:, cols].T
        k_tile = k_ref[:, cols]
        for natural, to, at, odd in users:
            part = slice(odd * head_size, (odd + 1) * head_size)
            z, p = divmod(natural, chips_seq)
            to = to.at[p, z ^ me_ref[0], at]
            to[0] = jnp.concatenate([k_tile[:half, part], k_tile[half:, part]], axis=1)
            to[1] = v_t[part]
            to[2] = q_t[part]
    for kz in range(head_count):
        apart[-1 - kz][...] = held_one[:, kz]
    own[...] = held[:, 0]
    for kp in range(chips_seq):
        rows = joined[kp].shape[0] - lists.shape[0]
        joined[kp][:rows] = held[me_ref[1] ^ kp, 1:].reshape(rows, tokens)
        joined[kp][rows:] = lists


def list_rows(heads):
    return pl.cdiv(heads, 16) * 16


def pack(me, queries, keys, values, lists, used, *, chips_seq, head_count, per_chip, head_size):
    tokens, width = queries.shape
    whole = pl.BlockSpec((tokens, width), lambda i, me: (0, 0))
    single, paired = (per_chip - 1,), tuple(range(per_chip - 1))
    part = (3, head_size, tokens)
    shapes = [(chips_seq, 1, *part)] * head_count
    shapes.append((chips_seq, len(paired), *part))
    rows = (head_count - 1) * len(paired) * math.prod(part[:-1]) + list_rows(lists.shape[2])
    shapes += [(rows, tokens)] * chips_seq
    return pl.pallas_call(
        functools.partial(
            pack_kernel,
            single=single, paired=paired,
            chips_seq=chips_seq, head_count=head_count, per_chip=per_chip,
        ),
        grid_spec=pltpu.PrefetchScalarGridSpec(
            num_scalar_prefetch=1,
            grid=(1,),
            in_specs=[
                *[whole] * 3,
                pl.BlockSpec(lists.shape, lambda i, me: (0, 0, 0)),
                pl.BlockSpec(used.shape, lambda i, me: (0, 0)),
            ],
            out_specs=[pl.BlockSpec(s, lambda i, me, n=len(s): (0,) * n) for s in shapes],
            scratch_shapes=[
                pltpu.VMEM((chips_seq, head_count, len(heads), *part), queries.dtype)
                for heads in (single, paired)
            ]
            + [pltpu.VMEM((tokens, tokens), jnp.float32)],
        ),
        out_shape=[jax.ShapeDtypeStruct(s, queries.dtype) for s in shapes],
        compiler_params=pltpu.CompilerParams(vmem_limit_bytes=48 << 20),
        name="pack",
    )(me, queries, keys, values, lists, used)


def attend_kernel(
    me_ref, table_ref, *rest, scale, entries, chips_seq, head_count, per_chip, j, near
):
    mine, other = rest[:head_count], rest[head_count : 2 * head_count]
    out_ref, q, kv = rest[-3:]
    blocks, head_size, tokens = q.shape
    paired = per_chip // 2 * 2
    head = me_ref[1] * paired + j if j < paired else chips_seq * paired + me_ref[1]
    head = head + pl.program_id(0)
    most = entries - 1
    for kz in range(head_count):
        for p in range(chips_seq):
            natural = (me_ref[0] ^ kz) * chips_seq + (p ^ me_ref[1] if near and kz else p)
            q[natural] = mine[kz][p, 0, 2]
            kv[natural] = mine[kz][p, 0, :2]
            kv[blocks + natural] = other[kz][p, 0]
    ones = jnp.ones((SUM_ROWS, tokens), jnp.bfloat16)
    zeros = jnp.zeros((head_size, tokens), jnp.bfloat16)

    def row_of(base, r):
        return r % chips_seq ^ me_ref[1], base // chips_seq + r // chips_seq

    def rows_of(base, counts, seen):
        scores, values = [], []
        for r in range(ROWS):
            p, z = row_of(base, r)
            own = base + r
            q_t = q[own]
            both = [jnp.concatenate([q_t, zeros], axis=1), jnp.concatenate([zeros, q_t], axis=1)]
            keys, vals = [kv[own, 0]], [jnp.concatenate([kv[own, 1], ones], axis=0)]
            for e in range(1, seen):
                live = e <= counts[r]
                slot = jnp.where(live, table_ref[p, head, z * most + e - 1], own)
                factor = jnp.where(live, 1.0, 0.0).astype(jnp.bfloat16)
                keys.append(kv[slot, 0])
                vals.append(jnp.concatenate([kv[slot, 1], ones], axis=0) * factor)
            scores.append(
                jnp.dot(
                    jnp.concatenate(keys, axis=0),
                    jnp.concatenate(both, axis=0),
                    preferred_element_type=jnp.float32,
                )
            )
            values.append(jnp.concatenate(vals, axis=1))
        for r in range(ROWS):
            top = jnp.max(scores[r], axis=0, keepdims=True)
            top = jnp.maximum(top[:, :tokens], top[:, tokens:])
            top = jnp.concatenate([top, top], axis=1)
            probs = jnp.exp2((scores[r] - top) * scale).astype(jnp.bfloat16)
            probs = [
                probs[e * head_size : (e + 1) * head_size, c * tokens : (c + 1) * tokens]
                for e in range(seen)
                for c in range(2)
            ]
            total = jnp.dot(
                values[r], jnp.concatenate(probs, axis=0), preferred_element_type=jnp.float32
            )
            out_ref[base + r, 0] = (total[:head_size] / total[head_size : head_size + 1]).astype(
                out_ref.dtype
            )

    def group(g, carry):
        base = g * ROWS
        counts = []
        for r in range(ROWS):
            p, z = row_of(base, r)
            counts.append(table_ref[p, head, head_count * most + z])
        seen = 1 + functools.reduce(jnp.maximum, counts)
        below = 0
        for size in (*range(3, entries, 2), entries):
            pl.when((seen > below) & (seen <= size))(
                functools.partial(rows_of, base, counts, size)
            )
            below = size
        return carry

    lax.fori_loop(0, blocks // ROWS, group, 0)


def attend(
    me, table, mine, other, held, *, entries, j, near, per_chip, chips_seq, head_count
):
    blocks = chips_seq * head_count
    block = mine[0][0].shape[-2:]
    head_size, tokens = block

    def spec(at, parts):
        return pl.BlockSpec((chips_seq, 1, parts, *block), lambda i, *_: (0, at + i, 0, 0, 0))

    in_specs = [spec(at, 3) for _, at in mine] + [spec(at, 2) for _, at in other]
    operands = [me, table] + [array for array, _ in mine + other]
    dtype = mine[0][0].dtype
    aliases = {}
    if held is not None:
        in_specs.append(pl.BlockSpec(memory_space=pl.ANY))
        aliases = {len(operands): 0}
        operands.append(held)
    return pl.pallas_call(
        functools.partial(
            attend_kernel,
            scale=LOG2E / math.sqrt(head_size), entries=entries,
            chips_seq=chips_seq, head_count=head_count, per_chip=per_chip, j=j, near=near,
        ),
        grid_spec=pltpu.PrefetchScalarGridSpec(
            num_scalar_prefetch=2,
            grid=(mine[-1][0].shape[1] - mine[-1][1],) if near else (1,),
            in_specs=in_specs,
            out_specs=pl.BlockSpec((blocks, 1, *block), lambda i, *_: (0, j + i, 0, 0)),
            scratch_shapes=[
                pltpu.VMEM((blocks, *block), dtype),
                pltpu.VMEM((2 * blocks, 2, *block), dtype),
            ],
        ),
        out_shape=jax.ShapeDtypeStruct((blocks, per_chip, *block), dtype),
        input_output_aliases=aliases,
        compiler_params=pltpu.CompilerParams(vmem_limit_bytes=48 << 20),
        cost_estimate=pl.CostEstimate(flops=1, transcendentals=1, bytes_accessed=1),
        name="attend",
    )(*operands)


def sync(*values):
    return lax.optimization_barrier(values)


def swap(value, axis, k):
    size = lax.axis_size(axis)
    return lax.ppermute(value, axis, [(i, i ^ k) for i in range(size)])


def on_pair(projected, key_lists, list_counts, *, chips_seq, head_count):
    tokens, _, width = projected.shape
    heads_dev, blocks_dev, list_most = key_lists.shape
    head_size = width // (heads_dev * head_count)
    per_chip = heads_dev // chips_seq
    entries = 1 + list_most
    me = jnp.stack([lax.axis_index(a) for a in ("head", "chip", "core")]).astype(jnp.int32)

    qkv = projected[:, 0], projected[:, 1], projected[:, 2]
    sizes = dict(chips_seq=chips_seq, head_count=head_count, per_chip=per_chip)

    def over(parts, axis, name):
        with jax.named_scope(name):
            return [parts[0]] + [swap(parts[k], axis, k) for k in reversed(range(1, len(parts)))][::-1]

    def over_p(value, name):
        with jax.named_scope(name):
            return lax.all_to_all(value, "chip", split_axis=0, concat_axis=0, tiled=True)

    def over_cores(value, name):
        with jax.named_scope(name):
            return swap(value, "core", 1)

    def heads(c, mine, other, held, table, near):
        with jax.named_scope(f"heads{c}"):
            return attend(me, table, mine, other, held, entries=entries, j=c, near=near, **sizes)

    last, each = per_chip - 1, range(head_count)
    packed = pack(me, *qkv, key_lists.transpose(1, 2, 0), list_counts.T, head_size=head_size, **sizes)
    singles, own, pairs = packed[head_count - 1 :: -1], packed[head_count], packed[head_count + 1 :]
    seen = list_counts[0, 0] > 0

    def last_head(singles, own, table):
        plane = over_p(jnp.concatenate([jnp.stack(singles, axis=1)[:, :, 0], own], axis=1), "plane")
        other = over_cores(plane, "cores2")
        held = heads(
            last, [(plane, kz) for kz in each], [(other, kz) for kz in each], None, table, False
        )
        return plane, other, held

    def none(*operands):
        shapes = jax.eval_shape(last_head, *operands)
        return jax.tree.map(lambda s: jnp.zeros(s.shape, s.dtype), shapes)

    pairs = over(pairs, "chip", "p01")
    singles = over(singles, "head", "z2")
    rows = pairs[0].shape[0] - list_rows(heads_dev)
    table = jnp.stack([part[rows:] for part in pairs]).astype(jnp.int32)
    shape = (head_count - 1, per_chip - 1, 3, head_size, tokens)
    pairs = [part[:rows].reshape(shape) for part in pairs]
    with jax.named_scope("z01"):
        rest_sent = [
            jnp.stack([part[k - 1] for part in pairs]) for k in reversed(range(1, head_count))
        ][::-1]
        rest = [swap(rest_sent[k - 1], "head", k) for k in reversed(range(1, head_count))][::-1]
    singles = sync(singles, rest_sent)[0]
    plane, other, held = lax.cond(seen, last_head, none, singles, own, table)
    rest = [sync(part, held)[0] for part in rest]
    mine = [(plane, head_count)] + [(part, 0) for part in rest]
    other = [(other, head_count)] + [(over_cores(part, "cores01"), 0) for part in rest]
    held = heads(0, mine, other, held, table, True)
    back = lax.all_to_all(held, ("head", "chip"), split_axis=0, concat_axis=0, tiled=True)
    back = back.reshape(head_count, chips_seq, per_chip, head_size, tokens)
    paired = per_chip // 2 * 2
    back = jnp.concatenate(
        [
            back[:, :, :paired].reshape(head_count, chips_seq * paired, head_size, tokens),
            back[:, :, paired:].reshape(head_count, -1, head_size, tokens),
        ],
        axis=1,
    )
    return back.reshape(width, tokens).T


def attend_rows(query_part, gathered, live_cols, head_size):
    row_count, seen_blocks, block_len, doubled = gathered.shape
    key_rows = gathered[..., :head_size].reshape(row_count, seen_blocks * block_len, head_size)
    value_rows = gathered[..., head_size:].reshape(row_count, seen_blocks * block_len, head_size)
    attention_scores = jnp.einsum(
        "rqd,rkd->rqk", query_part, key_rows, preferred_element_type=jnp.float32
    ) * (1.0 / math.sqrt(head_size))
    attention_scores = attention_scores.reshape(row_count, block_len, seen_blocks, block_len)
    attention_scores = jnp.where(live_cols[:, None, :, None], attention_scores, NEG_FILL)
    row_top = jnp.max(attention_scores, axis=(2, 3), keepdims=True)
    exp_scores = jnp.exp(attention_scores - row_top)
    attention_weights = (exp_scores / jnp.sum(exp_scores, axis=(2, 3), keepdims=True)).astype(
        jnp.bfloat16
    )
    attention_weights = attention_weights.reshape(row_count, block_len, seen_blocks * block_len)
    return jnp.einsum(
        "rqk,rkd->rqd", attention_weights, value_rows, preferred_element_type=jnp.float32
    )


def on_device(projected, key_lists, list_counts):
    seq_count = lax.axis_size("seq")
    heads_dev, blocks_dev, list_most = key_lists.shape
    regrouped = lax.all_to_all(projected, "head", split_axis=2, concat_axis=0, tiled=True)
    block_len = regrouped.shape[0] // blocks_dev
    group_width = regrouped.shape[2]
    head_size = group_width // heads_dev
    row_count = heads_dev * blocks_dev
    splitted = regrouped.reshape(blocks_dev, block_len, 3, heads_dev, head_size)
    queries = splitted[:, :, 0].transpose(2, 0, 1, 3).reshape(row_count, block_len, head_size)
    kv_pairs = jnp.concatenate([splitted[:, :, 1], splitted[:, :, 2]], axis=-1)
    kv_pairs = kv_pairs.transpose(2, 0, 1, 3).reshape(row_count, block_len, 2 * head_size)
    entries = key_lists.reshape(row_count * list_most)
    owners = entries // blocks_dev
    row_head = jnp.arange(row_count * list_most, dtype=jnp.int32) // (blocks_dev * list_most)
    capacity = row_count * list_most // seq_count
    wanted = row_head * blocks_dev + entries % blocks_dev
    onehot = (owners[:, None] == jnp.arange(seq_count, dtype=jnp.int32)[None, :]).astype(jnp.int32)
    within = jnp.sum(onehot * (jnp.cumsum(onehot, axis=0) - 1), axis=1)
    slot_ids = owners * capacity + within
    request = (
        jnp.zeros((seq_count * capacity,), jnp.int32)
        .at[slot_ids]
        .set(wanted)
        .reshape(seq_count, capacity)
    )
    asked_for = lax.all_to_all(request, "seq", split_axis=0, concat_axis=0, tiled=True)
    served = jnp.take(kv_pairs, asked_for.reshape(-1), axis=0).reshape(
        seq_count, capacity, block_len, 2 * head_size
    )
    fetched = lax.all_to_all(served, "seq", split_axis=0, concat_axis=0, tiled=True)
    fetched = fetched.reshape(seq_count * capacity, block_len, 2 * head_size)
    entry_slots = slot_ids.reshape(row_count, list_most)
    row_counts = list_counts.reshape(row_count)
    group_rows = 4

    def one_group(group_index):
        start = group_index * group_rows
        query_part = lax.dynamic_slice_in_dim(queries, start, group_rows, 0)
        own_pairs = lax.dynamic_slice_in_dim(kv_pairs, start, group_rows, 0)
        slot_part = lax.dynamic_slice_in_dim(entry_slots, start, group_rows, 0)
        count_part = lax.dynamic_slice_in_dim(row_counts, start, group_rows, 0)
        listed = jnp.take(fetched, slot_part.reshape(-1), axis=0).reshape(
            group_rows, list_most, block_len, 2 * head_size
        )
        gathered = jnp.concatenate([own_pairs[:, None], listed], axis=1)
        live_cols = jnp.concatenate(
            [
                jnp.ones((group_rows, 1), bool),
                jnp.arange(list_most, dtype=jnp.int32)[None, :] < count_part[:, None],
            ],
            axis=1,
        )
        return attend_rows(query_part, gathered, live_cols, head_size).astype(jnp.bfloat16)

    attended = lax.map(one_group, jnp.arange(row_count // group_rows, dtype=jnp.int32))
    attended = attended.reshape(row_count, block_len, head_size)
    laid_out = attended.reshape(heads_dev, blocks_dev * block_len, head_size).transpose(1, 0, 2)
    laid_out = laid_out.reshape(blocks_dev * block_len, group_width)
    return lax.all_to_all(laid_out, "head", split_axis=0, concat_axis=1, tiled=True)


def whole_heads_fit(mesh, projected, key_lists):
    seq_count, head_count = mesh.shape["seq"], mesh.shape["head"]
    if seq_count % PAIR:
        return False
    chips_seq = seq_count // PAIR
    chips = chips_seq * head_count
    group_heads = key_lists.shape[0] // head_count
    one_block = key_lists.shape[1] == seq_count * head_count
    powers = all(n & (n - 1) == 0 for n in (chips_seq, head_count))
    if not (one_block and powers and group_heads % chips_seq == 0 and chips % ROWS == 0):
        return False
    small = max(PAIR * chips, key_lists.shape[2]) <= 256
    odd = (group_heads // chips_seq) % 2 == 1
    tokens = projected.shape[0] // (seq_count * head_count)
    fit = head_count * (key_lists.shape[2] + 1) <= tokens and group_heads <= tokens
    return small and odd and fit and chips_seq % 2 == 0 and ROWS % chips_seq == 0


def solution(mesh):
    seq_count, head_count = mesh.shape["seq"], mesh.shape["head"]

    def run(projected, key_lists, list_counts):
        if not whole_heads_fit(mesh, projected, key_lists):
            return jax.shard_map(
                on_device,
                mesh=mesh,
                in_specs=(P(("seq", "head"), None, None), P("head", "seq", None), P("head", "seq")),
                out_specs=P(("seq", "head"), None),
                check_vma=False,
            )(projected, key_lists, list_counts)
        chips_seq = seq_count // PAIR
        split = Mesh(mesh.devices.reshape(chips_seq, PAIR, head_count), ("chip", "core", "head"))
        seq = ("chip", "core")
        return jax.shard_map(
            functools.partial(on_pair, chips_seq=chips_seq, head_count=head_count),
            mesh=split,
            in_specs=(P(seq + ("head",), None, None), P("head", seq, None), P("head", seq)),
            out_specs=P(seq + ("head",), None),
            check_vma=False,
        )(projected, key_lists, list_counts)

    return run
```

```python
import functools
import math

import jax
import jax.numpy as jnp
from jax import lax
from jax.experimental import pallas as pl
from jax.experimental.pallas import tpu as pltpu
from jax.sharding import Mesh
from jax.sharding import PartitionSpec as P

NEG_FILL = -1e30
LOG2E = 1.4426950408889634
PAIR = 2
ROWS = 8
SUM_ROWS = 16


def head_of(natural, j, chips_seq, per_chip):
    z, p = divmod(natural, chips_seq)
    paired = per_chip // 2 * 2
    group = z * chips_seq * per_chip
    if j < paired:
        return group + p * paired + j
    return group + chips_seq * paired + p


def pack_kernel(
    me_ref, q_ref, k_ref, v_ref, lists_ref, used_ref, *rest,
    single, paired, chips_seq, head_count, per_chip
):
    apart, own, joined = rest[:head_count], rest[head_count], rest[head_count + 1 : -3]
    held_one, held, table = rest[-3:]
    blocks, list_most, heads = lists_ref.shape
    table[...] = jnp.zeros_like(table)
    for b in range(blocks):
        listed = lists_ref[b]
        shard = listed // head_count
        slots = (shard % PAIR != me_ref[2]).astype(jnp.int32) * (chips_seq * head_count)
        slots += listed % head_count * chips_seq + shard // PAIR
        table[b * list_most : (b + 1) * list_most, :heads] = slots.astype(jnp.float32)
    table[blocks * list_most : blocks * (list_most + 1), :heads] = used_ref[...].astype(jnp.float32)
    lists = table[...].T[: list_rows(heads)].astype(joined[0].dtype)
    tokens = q_ref.shape[0]
    head_size = held.shape[-2]
    half, lanes = tokens // 2, 2 * head_size
    places = {}
    for natural in range(chips_seq * head_count):
        for to, heads in ((held_one, single), (held, paired)):
            for at, j in enumerate(heads):
                tile, odd = divmod(head_of(natural, j, chips_seq, per_chip), 2)
                places.setdefault(tile, []).append((natural, to, at, odd))
    for tile, users in places.items():
        cols = slice(tile * lanes, (tile + 1) * lanes)
        q_t = q_ref[:, cols].T
        v_t = v_ref[:, cols].T
        k_tile = k_ref[:, cols]
        for natural, to, at, odd in users:
            part = slice(odd * head_size, (odd + 1) * head_size)
            z, p = divmod(natural, chips_seq)
            to = to.at[p, z ^ me_ref[0], at]
            to[0] = jnp.concatenate([k_tile[:half, part], k_tile[half:, part]], axis=1)
            to[1] = v_t[part]
            to[2] = q_t[part]
    for kz in range(head_count):
        apart[-1 - kz][...] = held_one[:, kz]
    own[...] = held[:, 0]
    for kp in range(chips_seq):
        rows = joined[kp].shape[0] - lists.shape[0]
        joined[kp][:rows] = held[me_ref[1] ^ kp, 1:].reshape(rows, tokens)
        joined[kp][rows:] = lists


def list_rows(heads):
    return pl.cdiv(heads, 16) * 16


def pack(me, queries, keys, values, lists, used, *, chips_seq, head_count, per_chip, head_size):
    tokens, width = queries.shape
    whole = pl.BlockSpec((tokens, width), lambda i, me: (0, 0))
    single, paired = (per_chip - 1,), tuple(range(per_chip - 1))
    part = (3, head_size, tokens)
    shapes = [(chips_seq, 1, *part)] * head_count
    shapes.append((chips_seq, len(paired), *part))
    rows = (head_count - 1) * len(paired) * math.prod(part[:-1]) + list_rows(lists.shape[2])
    shapes += [(rows, tokens)] * chips_seq
    return pl.pallas_call(
        functools.partial(
            pack_kernel,
            single=single, paired=paired,
            chips_seq=chips_seq, head_count=head_count, per_chip=per_chip,
        ),
        grid_spec=pltpu.PrefetchScalarGridSpec(
            num_scalar_prefetch=1,
            grid=(1,),
            in_specs=[
                *[whole] * 3,
                pl.BlockSpec(lists.shape, lambda i, me: (0, 0, 0)),
                pl.BlockSpec(used.shape, lambda i, me: (0, 0)),
            ],
            out_specs=[pl.BlockSpec(s, lambda i, me, n=len(s): (0,) * n) for s in shapes],
            scratch_shapes=[
                pltpu.VMEM((chips_seq, head_count, len(heads), *part), queries.dtype)
                for heads in (single, paired)
            ]
            + [pltpu.VMEM((tokens, tokens), jnp.float32)],
        ),
        out_shape=[jax.ShapeDtypeStruct(s, queries.dtype) for s in shapes],
        compiler_params=pltpu.CompilerParams(vmem_limit_bytes=48 << 20),
        name="pack",
    )(me, queries, keys, values, lists, used)


def attend_kernel(
    me_ref, table_ref, *rest, scale, entries, chips_seq, head_count, per_chip, j, near
):
    mine, other = rest[:head_count], rest[head_count : 2 * head_count]
    out_ref, q, kv = rest[-3:]
    blocks, head_size, tokens = q.shape
    paired = per_chip // 2 * 2
    head = me_ref[1] * paired + j if j < paired else chips_seq * paired + me_ref[1]
    head = head + pl.program_id(0)
    most = entries - 1
    for kz in range(head_count):
        for p in range(chips_seq):
            natural = (me_ref[0] ^ kz) * chips_seq + (p ^ me_ref[1] if near and kz else p)
            q[natural] = mine[kz][p, 0, 2]
            kv[natural] = mine[kz][p, 0, :2]
            kv[blocks + natural] = other[kz][p, 0]
    ones = jnp.ones((SUM_ROWS, tokens), jnp.bfloat16)
    zeros = jnp.zeros((head_size, tokens), jnp.bfloat16)

    def row_of(base, r):
        return r % chips_seq ^ me_ref[1], base // chips_seq + r // chips_seq

    def rows_of(base, counts, seen):
        scores, values = [], []
        for r in range(ROWS):
            p, z = row_of(base, r)
            own = base + r
            q_t = q[own]
            both = [jnp.concatenate([q_t, zeros], axis=1), jnp.concatenate([zeros, q_t], axis=1)]
            keys, vals = [kv[own, 0]], [jnp.concatenate([kv[own, 1], ones], axis=0)]
            for e in range(1, seen):
                live = e <= counts[r]
                slot = jnp.where(live, table_ref[p, head, z * most + e - 1], own)
                factor = jnp.where(live, 1.0, 0.0).astype(jnp.bfloat16)
                keys.append(kv[slot, 0])
                vals.append(jnp.concatenate([kv[slot, 1], ones], axis=0) * factor)
            scores.append(
                jnp.dot(
                    jnp.concatenate(keys, axis=0),
                    jnp.concatenate(both, axis=0),
                    preferred_element_type=jnp.float32,
                )
            )
            values.append(jnp.concatenate(vals, axis=1))
        for r in range(ROWS):
            top = jnp.max(scores[r], axis=0, keepdims=True)
            top = jnp.maximum(top[:, :tokens], top[:, tokens:])
            top = jnp.concatenate([top, top], axis=1)
            probs = jnp.exp2((scores[r] - top) * scale).astype(jnp.bfloat16)
            probs = [
                probs[e * head_size : (e + 1) * head_size, c * tokens : (c + 1) * tokens]
                for e in range(seen)
                for c in range(2)
            ]
            total = jnp.dot(
                values[r], jnp.concatenate(probs, axis=0), preferred_element_type=jnp.float32
            )
            out_ref[base + r, 0] = (total[:head_size] / total[head_size : head_size + 1]).astype(
                out_ref.dtype
            )

    def group(g, carry):
        base = g * ROWS
        counts = []
        for r in range(ROWS):
            p, z = row_of(base, r)
            counts.append(table_ref[p, head, head_count * most + z])
        seen = 1 + functools.reduce(jnp.maximum, counts)
        below = 0
        for size in (*range(3, entries, 2), entries):
            pl.when((seen > below) & (seen <= size))(
                functools.partial(rows_of, base, counts, size)
            )
            below = size
        return carry

    lax.fori_loop(0, blocks // ROWS, group, 0)


def attend(me, table, mine, other, *, entries, j, near, per_chip, chips_seq, head_count):
    blocks = chips_seq * head_count
    block = mine[0][0].shape[-2:]
    head_size, tokens = block

    def spec(at, parts):
        return pl.BlockSpec((chips_seq, 1, parts, *block), lambda i, *_: (0, at + i, 0, 0, 0))

    in_specs = [spec(at, 3) for _, at in mine] + [spec(at, 2) for _, at in other]
    operands = [me, table] + [array for array, _ in mine + other]
    dtype = mine[0][0].dtype
    count = mine[-1][0].shape[1] - mine[-1][1] if near else 1
    return pl.pallas_call(
        functools.partial(
            attend_kernel,
            scale=LOG2E / math.sqrt(head_size), entries=entries,
            chips_seq=chips_seq, head_count=head_count, per_chip=per_chip, j=j, near=near,
        ),
        grid_spec=pltpu.PrefetchScalarGridSpec(
            num_scalar_prefetch=2,
            grid=(count,),
            in_specs=in_specs,
            out_specs=pl.BlockSpec((blocks, 1, *block), lambda i, *_: (0, i, 0, 0)),
            scratch_shapes=[
                pltpu.VMEM((blocks, *block), dtype),
                pltpu.VMEM((2 * blocks, 2, *block), dtype),
            ],
        ),
        out_shape=jax.ShapeDtypeStruct((blocks, count, *block), dtype),
        compiler_params=pltpu.CompilerParams(vmem_limit_bytes=48 << 20),
        cost_estimate=pl.CostEstimate(flops=1, transcendentals=1, bytes_accessed=1),
        name="attend",
    )(*operands)


def sync(*values):
    return lax.optimization_barrier(values)


def swap(value, axis, k):
    size = lax.axis_size(axis)
    return lax.ppermute(value, axis, [(i, i ^ k) for i in range(size)])


def on_pair(projected, key_lists, list_counts, *, chips_seq, head_count):
    tokens, _, width = projected.shape
    heads_dev, blocks_dev, list_most = key_lists.shape
    head_size = width // (heads_dev * head_count)
    per_chip = heads_dev // chips_seq
    entries = 1 + list_most
    me = jnp.stack([lax.axis_index(a) for a in ("head", "chip", "core")]).astype(jnp.int32)

    qkv = projected[:, 0], projected[:, 1], projected[:, 2]
    sizes = dict(chips_seq=chips_seq, head_count=head_count, per_chip=per_chip)

    def over(parts, axis, name):
        with jax.named_scope(name):
            return [parts[0]] + [swap(parts[k], axis, k) for k in reversed(range(1, len(parts)))][::-1]

    def over_p(value, name):
        with jax.named_scope(name):
            return lax.all_to_all(value, "chip", split_axis=0, concat_axis=0, tiled=True)

    def over_cores(value, name):
        with jax.named_scope(name):
            return swap(value, "core", 1)

    def heads(c, mine, other, table, near):
        with jax.named_scope(f"heads{c}"):
            return attend(me, table, mine, other, entries=entries, j=c, near=near, **sizes)

    last, each = per_chip - 1, range(head_count)
    packed = pack(me, *qkv, key_lists.transpose(1, 2, 0), list_counts.T, head_size=head_size, **sizes)
    singles, own, pairs = packed[head_count - 1 :: -1], packed[head_count], packed[head_count + 1 :]
    seen = list_counts[0, 0] > 0

    def last_head(singles, own, table):
        plane = over_p(jnp.concatenate([jnp.stack(singles, axis=1)[:, :, 0], own], axis=1), "plane")
        other = over_cores(plane, "cores2")
        held = heads(
            last, [(plane, kz) for kz in each], [(other, kz) for kz in each], table, False
        )
        return plane, other, held

    def none(*operands):
        shapes = jax.eval_shape(last_head, *operands)
        return jax.tree.map(lambda s: jnp.zeros(s.shape, s.dtype), shapes)

    pairs = over(pairs, "chip", "p01")
    singles = over(singles, "head", "z2")
    rows = pairs[0].shape[0] - list_rows(heads_dev)
    table = jnp.stack([part[rows:] for part in pairs]).astype(jnp.int32)
    shape = (head_count - 1, per_chip - 1, 3, head_size, tokens)
    pairs = [part[:rows].reshape(shape) for part in pairs]
    with jax.named_scope("z01"):
        rest_sent = [
            jnp.stack([part[k - 1] for part in pairs]) for k in reversed(range(1, head_count))
        ][::-1]
        rest = [swap(rest_sent[k - 1], "head", k) for k in reversed(range(1, head_count))][::-1]
    singles = sync(singles, rest_sent)[0]
    plane, other, held = lax.cond(seen, last_head, none, singles, own, table)
    rest = [sync(part, held)[0] for part in rest]
    mine = [(plane, head_count)] + [(part, 0) for part in rest]
    other = [(other, head_count)] + [(over_cores(part, "cores01"), 0) for part in rest]
    held = [heads(0, mine, other, table, True), held]
    held = [
        lax.all_to_all(part, ("head", "chip"), split_axis=0, concat_axis=0, tiled=True)
        for part in held
    ]
    back = jnp.concatenate(
        [part.reshape(head_count, -1, head_size, tokens) for part in held], axis=1
    )
    return back.reshape(width, tokens).T


def attend_rows(query_part, gathered, live_cols, head_size):
    row_count, seen_blocks, block_len, doubled = gathered.shape
    key_rows = gathered[..., :head_size].reshape(row_count, seen_blocks * block_len, head_size)
    value_rows = gathered[..., head_size:].reshape(row_count, seen_blocks * block_len, head_size)
    attention_scores = jnp.einsum(
        "rqd,rkd->rqk", query_part, key_rows, preferred_element_type=jnp.float32
    ) * (1.0 / math.sqrt(head_size))
    attention_scores = attention_scores.reshape(row_count, block_len, seen_blocks, block_len)
    attention_scores = jnp.where(live_cols[:, None, :, None], attention_scores, NEG_FILL)
    row_top = jnp.max(attention_scores, axis=(2, 3), keepdims=True)
    exp_scores = jnp.exp(attention_scores - row_top)
    attention_weights = (exp_scores / jnp.sum(exp_scores, axis=(2, 3), keepdims=True)).astype(
        jnp.bfloat16
    )
    attention_weights = attention_weights.reshape(row_count, block_len, seen_blocks * block_len)
    return jnp.einsum(
        "rqk,rkd->rqd", attention_weights, value_rows, preferred_element_type=jnp.float32
    )


def on_device(projected, key_lists, list_counts):
    seq_count = lax.axis_size("seq")
    heads_dev, blocks_dev, list_most = key_lists.shape
    regrouped = lax.all_to_all(projected, "head", split_axis=2, concat_axis=0, tiled=True)
    block_len = regrouped.shape[0] // blocks_dev
    group_width = regrouped.shape[2]
    head_size = group_width // heads_dev
    row_count = heads_dev * blocks_dev
    splitted = regrouped.reshape(blocks_dev, block_len, 3, heads_dev, head_size)
    queries = splitted[:, :, 0].transpose(2, 0, 1, 3).reshape(row_count, block_len, head_size)
    kv_pairs = jnp.concatenate([splitted[:, :, 1], splitted[:, :, 2]], axis=-1)
    kv_pairs = kv_pairs.transpose(2, 0, 1, 3).reshape(row_count, block_len, 2 * head_size)
    entries = key_lists.reshape(row_count * list_most)
    owners = entries // blocks_dev
    row_head = jnp.arange(row_count * list_most, dtype=jnp.int32) // (blocks_dev * list_most)
    capacity = row_count * list_most // seq_count
    wanted = row_head * blocks_dev + entries % blocks_dev
    onehot = (owners[:, None] == jnp.arange(seq_count, dtype=jnp.int32)[None, :]).astype(jnp.int32)
    within = jnp.sum(onehot * (jnp.cumsum(onehot, axis=0) - 1), axis=1)
    slot_ids = owners * capacity + within
    request = (
        jnp.zeros((seq_count * capacity,), jnp.int32)
        .at[slot_ids]
        .set(wanted)
        .reshape(seq_count, capacity)
    )
    asked_for = lax.all_to_all(request, "seq", split_axis=0, concat_axis=0, tiled=True)
    served = jnp.take(kv_pairs, asked_for.reshape(-1), axis=0).reshape(
        seq_count, capacity, block_len, 2 * head_size
    )
    fetched = lax.all_to_all(served, "seq", split_axis=0, concat_axis=0, tiled=True)
    fetched = fetched.reshape(seq_count * capacity, block_len, 2 * head_size)
    entry_slots = slot_ids.reshape(row_count, list_most)
    row_counts = list_counts.reshape(row_count)
    group_rows = 4

    def one_group(group_index):
        start = group_index * group_rows
        query_part = lax.dynamic_slice_in_dim(queries, start, group_rows, 0)
        own_pairs = lax.dynamic_slice_in_dim(kv_pairs, start, group_rows, 0)
        slot_part = lax.dynamic_slice_in_dim(entry_slots, start, group_rows, 0)
        count_part = lax.dynamic_slice_in_dim(row_counts, start, group_rows, 0)
        listed = jnp.take(fetched, slot_part.reshape(-1), axis=0).reshape(
            group_rows, list_most, block_len, 2 * head_size
        )
        gathered = jnp.concatenate([own_pairs[:, None], listed], axis=1)
        live_cols = jnp.concatenate(
            [
                jnp.ones((group_rows, 1), bool),
                jnp.arange(list_most, dtype=jnp.int32)[None, :] < count_part[:, None],
            ],
            axis=1,
        )
        return attend_rows(query_part, gathered, live_cols, head_size).astype(jnp.bfloat16)

    attended = lax.map(one_group, jnp.arange(row_count // group_rows, dtype=jnp.int32))
    attended = attended.reshape(row_count, block_len, head_size)
    laid_out = attended.reshape(heads_dev, blocks_dev * block_len, head_size).transpose(1, 0, 2)
    laid_out = laid_out.reshape(blocks_dev * block_len, group_width)
    return lax.all_to_all(laid_out, "head", split_axis=0, concat_axis=1, tiled=True)


def whole_heads_fit(mesh, projected, key_lists):
    seq_count, head_count = mesh.shape["seq"], mesh.shape["head"]
    if seq_count % PAIR:
        return False
    chips_seq = seq_count // PAIR
    chips = chips_seq * head_count
    group_heads = key_lists.shape[0] // head_count
    one_block = key_lists.shape[1] == seq_count * head_count
    powers = all(n & (n - 1) == 0 for n in (chips_seq, head_count))
    if not (one_block and powers and group_heads % chips_seq == 0 and chips % ROWS == 0):
        return False
    small = max(PAIR * chips, key_lists.shape[2]) <= 256
    odd = (group_heads // chips_seq) % 2 == 1
    tokens = projected.shape[0] // (seq_count * head_count)
    fit = head_count * (key_lists.shape[2] + 1) <= tokens and group_heads <= tokens
    return small and odd and fit and group_heads > chips_seq and chips_seq % 2 == 0 and ROWS % chips_seq == 0


def solution(mesh):
    seq_count, head_count = mesh.shape["seq"], mesh.shape["head"]

    def run(projected, key_lists, list_counts):
        if not whole_heads_fit(mesh, projected, key_lists):
            return jax.shard_map(
                on_device,
                mesh=mesh,
                in_specs=(P(("seq", "head"), None, None), P("head", "seq", None), P("head", "seq")),
                out_specs=P(("seq", "head"), None),
                check_vma=False,
            )(projected, key_lists, list_counts)
        chips_seq = seq_count // PAIR
        split = Mesh(mesh.devices.reshape(chips_seq, PAIR, head_count), ("chip", "core", "head"))
        seq = ("chip", "core")
        return jax.shard_map(
            functools.partial(on_pair, chips_seq=chips_seq, head_count=head_count),
            mesh=split,
            in_specs=(P(seq + ("head",), None, None), P("head", seq, None), P("head", seq)),
            out_specs=P(seq + ("head",), None),
            check_vma=False,
        )(projected, key_lists, list_counts)

    return run
```

```python
import functools
import math

import jax
import jax.numpy as jnp
from jax import lax
from jax.experimental import pallas as pl
from jax.experimental.pallas import tpu as pltpu
from jax.sharding import Mesh
from jax.sharding import PartitionSpec as P

NEG_FILL = -1e30
LOG2E = 1.4426950408889634
PAIR = 2
ROWS = 8
SUM_ROWS = 16


def head_of(natural, j, chips_seq, per_chip):
    z, p = divmod(natural, chips_seq)
    paired = per_chip // 2 * 2
    group = z * chips_seq * per_chip
    if j < paired:
        return group + p * paired + j
    return group + chips_seq * paired + p


def pack_kernel(
    me_ref, q_ref, k_ref, v_ref, lists_ref, used_ref, *rest,
    single, paired, chips_seq, head_count, per_chip
):
    apart, own, joined = rest[:head_count], rest[head_count], rest[head_count + 1 : -3]
    held_one, held, table = rest[-3:]
    blocks, list_most, heads = lists_ref.shape
    table[...] = jnp.zeros_like(table)
    for b in range(blocks):
        listed = lists_ref[b]
        shard = listed // head_count
        slots = (shard % PAIR != me_ref[2]).astype(jnp.int32) * (chips_seq * head_count)
        slots += listed % head_count * chips_seq + shard // PAIR
        table[b * list_most : (b + 1) * list_most, :heads] = slots.astype(jnp.float32)
    table[blocks * list_most : blocks * (list_most + 1), :heads] = used_ref[...].astype(jnp.float32)
    lists = table[...].T[: list_rows(heads)].astype(joined[0].dtype)
    tokens = q_ref.shape[0]
    head_size = held.shape[-2]
    half, lanes = tokens // 2, 2 * head_size
    places = {}
    for natural in range(chips_seq * head_count):
        for to, heads in ((held_one, single), (held, paired)):
            for at, j in enumerate(heads):
                tile, odd = divmod(head_of(natural, j, chips_seq, per_chip), 2)
                places.setdefault(tile, []).append((natural, to, at, odd))
    for tile, users in places.items():
        cols = slice(tile * lanes, (tile + 1) * lanes)
        q_t = q_ref[:, cols].T
        v_t = v_ref[:, cols].T
        k_tile = k_ref[:, cols]
        for natural, to, at, odd in users:
            part = slice(odd * head_size, (odd + 1) * head_size)
            z, p = divmod(natural, chips_seq)
            to = to.at[p, z ^ me_ref[0], at]
            to[0] = jnp.concatenate([k_tile[:half, part], k_tile[half:, part]], axis=1)
            to[1] = v_t[part]
            to[2] = q_t[part]
    for kz in range(head_count):
        apart[-1 - kz][...] = held_one[:, kz]
    own[...] = held[:, 0]
    for kp in range(chips_seq):
        rows = joined[kp].shape[0] - lists.shape[0]
        joined[kp][:rows] = held[me_ref[1] ^ kp, 1:].reshape(rows, tokens)
        joined[kp][rows:] = lists


def list_rows(heads):
    return pl.cdiv(heads, 16) * 16


def pack(me, queries, keys, values, lists, used, *, chips_seq, head_count, per_chip, head_size):
    tokens, width = queries.shape
    whole = pl.BlockSpec((tokens, width), lambda i, me: (0, 0))
    single, paired = (per_chip - 1,), tuple(range(per_chip - 1))
    part = (3, head_size, tokens)
    shapes = [(chips_seq, 1, *part)] * head_count
    shapes.append((chips_seq, len(paired), *part))
    rows = (head_count - 1) * len(paired) * math.prod(part[:-1]) + list_rows(lists.shape[2])
    shapes += [(rows, tokens)] * chips_seq
    return pl.pallas_call(
        functools.partial(
            pack_kernel,
            single=single, paired=paired,
            chips_seq=chips_seq, head_count=head_count, per_chip=per_chip,
        ),
        grid_spec=pltpu.PrefetchScalarGridSpec(
            num_scalar_prefetch=1,
            grid=(1,),
            in_specs=[
                *[whole] * 3,
                pl.BlockSpec(lists.shape, lambda i, me: (0, 0, 0)),
                pl.BlockSpec(used.shape, lambda i, me: (0, 0)),
            ],
            out_specs=[pl.BlockSpec(s, lambda i, me, n=len(s): (0,) * n) for s in shapes],
            scratch_shapes=[
                pltpu.VMEM((chips_seq, head_count, len(heads), *part), queries.dtype)
                for heads in (single, paired)
            ]
            + [pltpu.VMEM((tokens, tokens), jnp.float32)],
        ),
        out_shape=[jax.ShapeDtypeStruct(s, queries.dtype) for s in shapes],
        compiler_params=pltpu.CompilerParams(vmem_limit_bytes=48 << 20),
        name="pack",
    )(me, queries, keys, values, lists, used)


def attend_kernel(
    me_ref, table_ref, *rest, scale, entries, chips_seq, head_count, per_chip, j, near
):
    mine, other = rest[:head_count], rest[head_count : 2 * head_count]
    out_ref, q, kv = rest[-3:]
    blocks, head_size, tokens = q.shape
    paired = per_chip // 2 * 2
    head = me_ref[1] * paired + j if j < paired else chips_seq * paired + me_ref[1]
    head = head + pl.program_id(0)
    most = entries - 1
    for kz in range(head_count):
        for p in range(chips_seq):
            natural = (me_ref[0] ^ kz) * chips_seq + (p ^ me_ref[1] if near and kz else p)
            q[natural] = mine[kz][p, 0, 2]
            kv[natural] = mine[kz][p, 0, :2]
            kv[blocks + natural] = other[kz][p, 0]
    ones = jnp.ones((SUM_ROWS, tokens), jnp.bfloat16)
    zeros = jnp.zeros((head_size, tokens), jnp.bfloat16)

    def row_of(base, r):
        return r % chips_seq ^ me_ref[1], base // chips_seq + r // chips_seq

    def rows_of(base, counts, seen):
        scores, values = [], []
        for r in range(ROWS):
            p, z = row_of(base, r)
            own = base + r
            q_t = q[own]
            both = [jnp.concatenate([q_t, zeros], axis=1), jnp.concatenate([zeros, q_t], axis=1)]
            keys, vals = [kv[own, 0]], [jnp.concatenate([kv[own, 1], ones], axis=0)]
            for e in range(1, seen):
                live = e <= counts[r]
                slot = jnp.where(live, table_ref[p, head, z * most + e - 1], own)
                factor = jnp.where(live, 1.0, 0.0).astype(jnp.bfloat16)
                keys.append(kv[slot, 0])
                vals.append(jnp.concatenate([kv[slot, 1], ones], axis=0) * factor)
            scores.append(
                jnp.dot(
                    jnp.concatenate(keys, axis=0),
                    jnp.concatenate(both, axis=0),
                    preferred_element_type=jnp.float32,
                )
            )
            values.append(jnp.concatenate(vals, axis=1))
        for r in range(ROWS):
            top = jnp.max(scores[r], axis=0, keepdims=True)
            top = jnp.maximum(top[:, :tokens], top[:, tokens:])
            top = jnp.concatenate([top, top], axis=1)
            probs = jnp.exp2((scores[r] - top) * scale).astype(jnp.bfloat16)
            probs = [
                probs[e * head_size : (e + 1) * head_size, c * tokens : (c + 1) * tokens]
                for e in range(seen)
                for c in range(2)
            ]
            total = jnp.dot(
                values[r], jnp.concatenate(probs, axis=0), preferred_element_type=jnp.float32
            )
            out_ref[base + r, 0] = (total[:head_size] / total[head_size : head_size + 1]).astype(
                out_ref.dtype
            )

    def group(g, carry):
        base = g * ROWS
        counts = []
        for r in range(ROWS):
            p, z = row_of(base, r)
            counts.append(table_ref[p, head, head_count * most + z])
        seen = 1 + functools.reduce(jnp.maximum, counts)
        below = 0
        for size in (*range(3, entries, 2), entries):
            pl.when((seen > below) & (seen <= size))(
                functools.partial(rows_of, base, counts, size)
            )
            below = size
        return carry

    lax.fori_loop(0, blocks // ROWS, group, 0)


def attend(me, table, mine, other, *, entries, j, near, per_chip, chips_seq, head_count):
    blocks = chips_seq * head_count
    block = mine[0][0].shape[-2:]
    head_size, tokens = block

    def spec(at, parts):
        return pl.BlockSpec((chips_seq, 1, parts, *block), lambda i, *_: (0, at + i, 0, 0, 0))

    in_specs = [spec(at, 3) for _, at in mine] + [spec(at, 2) for _, at in other]
    operands = [me, table] + [array for array, _ in mine + other]
    dtype = mine[0][0].dtype
    count = mine[-1][0].shape[1] - mine[-1][1] if near else 1
    return pl.pallas_call(
        functools.partial(
            attend_kernel,
            scale=LOG2E / math.sqrt(head_size), entries=entries,
            chips_seq=chips_seq, head_count=head_count, per_chip=per_chip, j=j, near=near,
        ),
        grid_spec=pltpu.PrefetchScalarGridSpec(
            num_scalar_prefetch=2,
            grid=(count,),
            in_specs=in_specs,
            out_specs=pl.BlockSpec((blocks, 1, *block), lambda i, *_: (0, i, 0, 0)),
            scratch_shapes=[
                pltpu.VMEM((blocks, *block), dtype),
                pltpu.VMEM((2 * blocks, 2, *block), dtype),
            ],
        ),
        out_shape=jax.ShapeDtypeStruct((blocks, count, *block), dtype),
        compiler_params=pltpu.CompilerParams(vmem_limit_bytes=48 << 20),
        cost_estimate=pl.CostEstimate(flops=1, transcendentals=1, bytes_accessed=1),
        name="attend",
    )(*operands)


def sync(*values):
    return lax.optimization_barrier(values)


def swap(value, axis, k):
    size = lax.axis_size(axis)
    return lax.ppermute(value, axis, [(i, i ^ k) for i in range(size)])


def on_pair(projected, key_lists, list_counts, *, chips_seq, head_count):
    tokens, _, width = projected.shape
    heads_dev, blocks_dev, list_most = key_lists.shape
    head_size = width // (heads_dev * head_count)
    per_chip = heads_dev // chips_seq
    entries = 1 + list_most
    me = jnp.stack([lax.axis_index(a) for a in ("head", "chip", "core")]).astype(jnp.int32)

    qkv = projected[:, 0], projected[:, 1], projected[:, 2]
    sizes = dict(chips_seq=chips_seq, head_count=head_count, per_chip=per_chip)

    def over(parts, axis, name):
        with jax.named_scope(name):
            return [parts[0]] + [swap(parts[k], axis, k) for k in reversed(range(1, len(parts)))][::-1]

    def over_p(value, name):
        with jax.named_scope(name):
            return lax.all_to_all(value, "chip", split_axis=0, concat_axis=0, tiled=True)

    def over_cores(value, name):
        with jax.named_scope(name):
            return swap(value, "core", 1)

    def heads(c, mine, other, table, near):
        with jax.named_scope(f"heads{c}"):
            return attend(me, table, mine, other, entries=entries, j=c, near=near, **sizes)

    last, each = per_chip - 1, range(head_count)
    packed = pack(me, *qkv, key_lists.transpose(1, 2, 0), list_counts.T, head_size=head_size, **sizes)
    singles, own, pairs = packed[head_count - 1 :: -1], packed[head_count], packed[head_count + 1 :]
    seen = list_counts[0, 0] > 0

    def last_head(singles, own, table):
        plane = over_p(jnp.concatenate([jnp.stack(singles, axis=1)[:, :, 0], own], axis=1), "plane")
        other = over_cores(plane, "cores2")
        held = heads(
            last, [(plane, kz) for kz in each], [(other, kz) for kz in each], table, False
        )
        return plane, other, held

    def none(*operands):
        shapes = jax.eval_shape(last_head, *operands)
        return jax.tree.map(lambda s: jnp.zeros(s.shape, s.dtype), shapes)

    pairs = over(pairs, "chip", "p01")
    singles = over(singles, "head", "z2")
    rows = pairs[0].shape[0] - list_rows(heads_dev)
    table = jnp.stack([part[rows:] for part in pairs]).astype(jnp.int32)
    shape = (head_count - 1, per_chip - 1, 3, head_size, tokens)
    pairs = [part[:rows].reshape(shape) for part in pairs]
    with jax.named_scope("z01"):
        rest_sent = [
            jnp.stack([part[k - 1] for part in pairs]) for k in reversed(range(1, head_count))
        ][::-1]
        rest = [swap(rest_sent[k - 1], "head", k) for k in reversed(range(1, head_count))][::-1]
    singles = sync(singles, rest_sent)[0]
    plane, other, held = lax.cond(seen, last_head, none, singles, own, table)
    rest = [sync(part, held)[0] for part in rest]
    mine = [(plane, head_count)] + [(part, 0) for part in rest]
    swapped = [over_cores(part, "cores01") for part in rest]
    held = sync(held, swapped)[0]
    other = [(other, head_count)] + [(part, 0) for part in swapped]
    held = [heads(0, mine, other, table, True), held]
    held = [
        lax.all_to_all(part, ("head", "chip"), split_axis=0, concat_axis=0, tiled=True)
        for part in held
    ]
    back = jnp.concatenate(
        [part.reshape(head_count, -1, head_size, tokens) for part in held], axis=1
    )
    return back.reshape(width, tokens).T


def attend_rows(query_part, gathered, live_cols, head_size):
    row_count, seen_blocks, block_len, doubled = gathered.shape
    key_rows = gathered[..., :head_size].reshape(row_count, seen_blocks * block_len, head_size)
    value_rows = gathered[..., head_size:].reshape(row_count, seen_blocks * block_len, head_size)
    attention_scores = jnp.einsum(
        "rqd,rkd->rqk", query_part, key_rows, preferred_element_type=jnp.float32
    ) * (1.0 / math.sqrt(head_size))
    attention_scores = attention_scores.reshape(row_count, block_len, seen_blocks, block_len)
    attention_scores = jnp.where(live_cols[:, None, :, None], attention_scores, NEG_FILL)
    row_top = jnp.max(attention_scores, axis=(2, 3), keepdims=True)
    exp_scores = jnp.exp(attention_scores - row_top)
    attention_weights = (exp_scores / jnp.sum(exp_scores, axis=(2, 3), keepdims=True)).astype(
        jnp.bfloat16
    )
    attention_weights = attention_weights.reshape(row_count, block_len, seen_blocks * block_len)
    return jnp.einsum(
        "rqk,rkd->rqd", attention_weights, value_rows, preferred_element_type=jnp.float32
    )


def on_device(projected, key_lists, list_counts):
    seq_count = lax.axis_size("seq")
    heads_dev, blocks_dev, list_most = key_lists.shape
    regrouped = lax.all_to_all(projected, "head", split_axis=2, concat_axis=0, tiled=True)
    block_len = regrouped.shape[0] // blocks_dev
    group_width = regrouped.shape[2]
    head_size = group_width // heads_dev
    row_count = heads_dev * blocks_dev
    splitted = regrouped.reshape(blocks_dev, block_len, 3, heads_dev, head_size)
    queries = splitted[:, :, 0].transpose(2, 0, 1, 3).reshape(row_count, block_len, head_size)
    kv_pairs = jnp.concatenate([splitted[:, :, 1], splitted[:, :, 2]], axis=-1)
    kv_pairs = kv_pairs.transpose(2, 0, 1, 3).reshape(row_count, block_len, 2 * head_size)
    entries = key_lists.reshape(row_count * list_most)
    owners = entries // blocks_dev
    row_head = jnp.arange(row_count * list_most, dtype=jnp.int32) // (blocks_dev * list_most)
    capacity = row_count * list_most // seq_count
    wanted = row_head * blocks_dev + entries % blocks_dev
    onehot = (owners[:, None] == jnp.arange(seq_count, dtype=jnp.int32)[None, :]).astype(jnp.int32)
    within = jnp.sum(onehot * (jnp.cumsum(onehot, axis=0) - 1), axis=1)
    slot_ids = owners * capacity + within
    request = (
        jnp.zeros((seq_count * capacity,), jnp.int32)
        .at[slot_ids]
        .set(wanted)
        .reshape(seq_count, capacity)
    )
    asked_for = lax.all_to_all(request, "seq", split_axis=0, concat_axis=0, tiled=True)
    served = jnp.take(kv_pairs, asked_for.reshape(-1), axis=0).reshape(
        seq_count, capacity, block_len, 2 * head_size
    )
    fetched = lax.all_to_all(served, "seq", split_axis=0, concat_axis=0, tiled=True)
    fetched = fetched.reshape(seq_count * capacity, block_len, 2 * head_size)
    entry_slots = slot_ids.reshape(row_count, list_most)
    row_counts = list_counts.reshape(row_count)
    group_rows = 4

    def one_group(group_index):
        start = group_index * group_rows
        query_part = lax.dynamic_slice_in_dim(queries, start, group_rows, 0)
        own_pairs = lax.dynamic_slice_in_dim(kv_pairs, start, group_rows, 0)
        slot_part = lax.dynamic_slice_in_dim(entry_slots, start, group_rows, 0)
        count_part = lax.dynamic_slice_in_dim(row_counts, start, group_rows, 0)
        listed = jnp.take(fetched, slot_part.reshape(-1), axis=0).reshape(
            group_rows, list_most, block_len, 2 * head_size
        )
        gathered = jnp.concatenate([own_pairs[:, None], listed], axis=1)
        live_cols = jnp.concatenate(
            [
                jnp.ones((group_rows, 1), bool),
                jnp.arange(list_most, dtype=jnp.int32)[None, :] < count_part[:, None],
            ],
            axis=1,
        )
        return attend_rows(query_part, gathered, live_cols, head_size).astype(jnp.bfloat16)

    attended = lax.map(one_group, jnp.arange(row_count // group_rows, dtype=jnp.int32))
    attended = attended.reshape(row_count, block_len, head_size)
    laid_out = attended.reshape(heads_dev, blocks_dev * block_len, head_size).transpose(1, 0, 2)
    laid_out = laid_out.reshape(blocks_dev * block_len, group_width)
    return lax.all_to_all(laid_out, "head", split_axis=0, concat_axis=1, tiled=True)


def whole_heads_fit(mesh, projected, key_lists):
    seq_count, head_count = mesh.shape["seq"], mesh.shape["head"]
    if seq_count % PAIR:
        return False
    chips_seq = seq_count // PAIR
    chips = chips_seq * head_count
    group_heads = key_lists.shape[0] // head_count
    one_block = key_lists.shape[1] == seq_count * head_count
    powers = all(n & (n - 1) == 0 for n in (chips_seq, head_count))
    if not (one_block and powers and group_heads % chips_seq == 0 and chips % ROWS == 0):
        return False
    small = max(PAIR * chips, key_lists.shape[2]) <= 256
    odd = (group_heads // chips_seq) % 2 == 1
    tokens = projected.shape[0] // (seq_count * head_count)
    fit = head_count * (key_lists.shape[2] + 1) <= tokens and group_heads <= tokens
    return small and odd and fit and group_heads > chips_seq and chips_seq % 2 == 0 and ROWS % chips_seq == 0


def solution(mesh):
    seq_count, head_count = mesh.shape["seq"], mesh.shape["head"]

    def run(projected, key_lists, list_counts):
        if not whole_heads_fit(mesh, projected, key_lists):
            return jax.shard_map(
                on_device,
                mesh=mesh,
                in_specs=(P(("seq", "head"), None, None), P("head", "seq", None), P("head", "seq")),
                out_specs=P(("seq", "head"), None),
                check_vma=False,
            )(projected, key_lists, list_counts)
        chips_seq = seq_count // PAIR
        split = Mesh(mesh.devices.reshape(chips_seq, PAIR, head_count), ("chip", "core", "head"))
        seq = ("chip", "core")
        return jax.shard_map(
            functools.partial(on_pair, chips_seq=chips_seq, head_count=head_count),
            mesh=split,
            in_specs=(P(seq + ("head",), None, None), P("head", seq, None), P("head", seq)),
            out_specs=P(seq + ("head",), None),
            check_vma=False,
        )(projected, key_lists, list_counts)

    return run
```
